32 devices in a mesh: dp: 4 (over z), expert: 2 (over y), tensor: 4 (over x, core).
Axes of the slice: x: 2, y: 2, z: 4, core: 2. Of those that a mesh axis runs over, the one named last changes fastest.
Arguments:
- layer_in: bfloat16 [2, 128, 4096], P(None, 'dp'), may hold values from -6 to 6
- conv_state: bfloat16 [128, 3, 4096], P('dp', None, ('expert', 'tensor')), may hold values from -6 to 6
- ssm_state: float32 [128, 16, 4096], P('dp', None, ('expert', 'tensor')), may hold values from -6 to 6
- proj_inner: bfloat16 [4096, 4096], P(None, ('expert', 'tensor')), may hold values from -0.09375 to 0.09375
- proj_gate: bfloat16 [4096, 4096], P(None, ('expert', 'tensor')), may hold values from -0.09375 to 0.09375
- conv_weight: float32 [4, 4096], P(None, ('expert', 'tensor')), may hold values from -3 to 3
- conv_bias: float32 [4096], P(('expert', 'tensor')), may hold values from -3 to 3
- delta_down: bfloat16 [4096, 256], P(('expert', 'tensor')), may hold values from -0.09375 to 0.09375
- state_proj: bfloat16 [2, 16, 4096], P(None, None, ('expert', 'tensor')), may hold values from -0.09375 to 0.09375
- delta_up: bfloat16 [256, 4096], P(None, ('expert', 'tensor')), may hold values from -0.375 to 0.375
- delta_bias: float32 [4096], P(('expert', 'tensor')), may hold values from -4 to -1
- decay_log: float32 [16, 4096], P(None, ('expert', 'tensor')), may hold values from 0 to 2.8
- skip_gain: float32 [4096], P(('expert', 'tensor')), may hold values from 0 to 2
- proj_out: bfloat16 [4096, 4096], P(('expert', 'tensor')), may hold values from -0.09375 to 0.09375
- expert_gate: bfloat16 [8, 8192, 4096], P('expert', ('dp', 'tensor')), may hold values from -0.09375 to 0.09375
- expert_up: bfloat16 [8, 8192, 4096], P('expert', ('dp', 'tensor')), may hold values from -0.09375 to 0.09375
- expert_down: bfloat16 [8, 8192, 4096], P('expert', ('dp', 'tensor')), may hold values from -0.0625 to 0.0625
- expert_ids: int32 [2, 128, 2], P(None, ('dp', 'expert', 'tensor')), may hold values from 0 to 7, all different within a row; in each aligned block of 4 rows (0 to 3, 4 to 7, ..., all dimensions but the last counted through in order) at most 2 rows name the same one
- route_weight: float32 [2, 128, 2], P(None, ('dp', 'expert', 'tensor')), may hold values from 0.2 to 1
Outputs:
- layer_out: bfloat16 [2, 128, 4096], P(None, ('dp', 'expert', 'tensor'))
- conv_final: bfloat16 [128, 3, 4096], P('dp', None, ('expert', 'tensor'))
- state_final: float32 [128, 16, 4096], P('dp', None, ('expert', 'tensor'))
The draws below stay inside these ranges and needn't reach their ends.
Inputs may be any that keep to these rules, and one draw needn't show every extreme that they name: `expert_ids`: in each decode step the 4 rows of one device (aligned blocks along the rows) name each expert at most 2 times, and in some devices' rows some expert is named exactly 2 times; the 2 experts of a row differ.
All inputs are finite; a program needn't handle non-finite values.
Results may differ from the reference program's by a relative error of at most 0.023.
Values may be sent and summed in bfloat16 or wider, within the bound.
No kernel may reach another device: no remote copies, remote signals or barrier semaphores. Data moves between devices by JAX's collectives and lax.ppermute only.
A program may use at most 128 MiB of HBM per device.

```python
import math
import jax
import jax.numpy as jnp
import numpy as np
from jax import lax

D = 4096
DI = 4096
N = 16
KC = 4
R = 256
EXPERTS = 8
TOP = 2
FF = 8192
STEPS = 2
ROW_DEV = 4
ROWS = 128
CAP = 2
N_DP = 4
N_EXPERT = 2
N_TENSOR = 4


def steps_of(own_key, extent, shards, smallest, high):
    loudness = 1.0
    for axis_at, parts in shards:
        steps = jax.random.uniform(jax.random.fold_in(jax.random.fold_in(own_key, 6), axis_at), (parts,), jnp.float32, smallest / len(shards), high / len(shards))
        loudness = loudness * jnp.repeat(jnp.exp(steps), extent[axis_at] // parts).reshape((-1,) + (1,) * (len(extent) - 1 - axis_at))
    return loudness


def routed_block(stream_key, own, number, rows, count, top, limit, lean):
    sequence = jax.random.permutation(stream_key, count)
    crowded, ordinary = load_shares(count, rows * top, limit, lean, True), load_shares(count, rows * top, limit, lean, False)
    places = jnp.arange(count)

    def named(lengths, offset_by):
        used = int((lengths > 0).sum())
        fixed = max(1, used // 4)
        shifted = fixed + (places - fixed + offset_by * (used - fixed)) % max(1, count - fixed)
        return jnp.zeros((count,), jnp.int32).at[sequence[jnp.where(places < fixed, places, shifted)]].set(jnp.asarray(lengths, jnp.int32))

    lengths = jnp.where(number % 4 == 0, named(crowded, number // 4), named(ordinary, number - number // 4 - 1))
    mixed = jax.random.permutation(jax.random.fold_in(own, 3), count)
    giver, taker = mixed[0:count // 2 * 2:2], mixed[1:count // 2 * 2:2]
    slack = jnp.minimum(lengths[giver] - 1, limit - lengths[taker]) // 2
    slack = jnp.where((giver == sequence[0]) | (taker == sequence[0]) | (lengths[taker] == 0), 0, jnp.maximum(slack, 0))
    shifted = jax.random.randint(jax.random.fold_in(own, 4), (count // 2,), 0, 1 << 20) % (slack + 1)
    lengths = lengths.at[giver].add(-shifted).at[taker].add(shifted)
    items = jnp.searchsorted(jnp.cumsum(lengths), jnp.arange(rows * top), side="right").astype(jnp.int32)
    grid = items.reshape(top, rows).T
    grid = grid[jax.random.permutation(jax.random.fold_in(own, 1), rows)]
    offset_by = jax.random.randint(jax.random.fold_in(own, 2), (rows, 1), 0, top)
    return jnp.take_along_axis(grid, (jnp.arange(top)[None, :] + offset_by) % top, axis=1)


def load_shares(count, total, limit, slope, full):
    weights = [(1 << 20) // math.isqrt(standing ** slope) + 1 for standing in range(1, count + 1)]
    largest = limit if full else min(limit, max(-(-total // count), total * weights[0] // sum(weights)))
    least = 1 if total - largest >= count - 1 else 0
    holding, spare = [largest] + [least] * (count - 1), total - largest - least * (count - 1)
    while spare > 0:
        movable = [i for i in range(1, count) if holding[i] < largest] or [i for i in range(1, count) if holding[i] < limit]
        whole, remaining = sum([weights[i] for i in movable]), spare
        for i in movable:
            extra = min(limit - holding[i], max(1, remaining * weights[i] // whole), spare)
            holding[i] = holding[i] + extra
            spare = spare - extra
    return np.array(holding)


def centred(key, shape, width, reach, pieces=(), kind=jnp.bfloat16):
    factor_of = steps_of(key, shape, pieces, -0.22, 0.18) if pieces else 1.0
    values = jax.random.normal(key, shape, jnp.float32) * width * factor_of
    return jnp.minimum(jnp.maximum(values, -reach), reach).astype(kind)


def setup_inputs(seed: int = 0) -> dict:
    splits = jax.random.split(jax.random.key(seed), 20)
    layer_in = centred(splits[0], (STEPS, ROWS, D), 1.0, 6.0, ((1, 4),))
    conv_state = centred(splits[1], (ROWS, KC - 1, DI), 1.0, 6.0, ((0, 4), (2, 8)))
    ssm_state = centred(splits[2], (ROWS, N, DI), 1.0, 6.0, ((0, 4), (2, 8)), jnp.float32)
    proj_inner = centred(splits[3], (D, DI), D ** -0.5, 0.09375, ((1, 8),))
    proj_gate = centred(splits[4], (D, DI), D ** -0.5, 0.09375, ((1, 8),))
    conv_weight = centred(splits[5], (KC, DI), KC ** -0.5, 3.0, ((1, 8),), jnp.float32)
    conv_bias = centred(splits[6], (DI,), 0.5, 3.0, ((0, 8),), jnp.float32)
    delta_down = centred(splits[7], (DI, R), DI ** -0.5, 0.09375, ((0, 8),))
    state_proj = centred(splits[8], (2, N, DI), DI ** -0.5, 0.09375, ((2, 8),))
    delta_up = centred(splits[9], (R, DI), R ** -0.5, 0.375, ((1, 8),))
    delta_bias = jnp.clip(-4.0 + 3.0 * jax.random.uniform(splits[10], (DI,), jnp.float32) ** steps_of(splits[10], (DI,), ((0, 8),), -0.2, 0.2), -4.0, -1.0)
    decay_log = jnp.clip(2.8 * jax.random.uniform(splits[11], (N, DI), jnp.float32) ** steps_of(splits[11], (N, DI), ((1, 8),), -0.2, 0.2), 0.0, 2.8)
    skip_gain = jnp.clip(2.0 * jax.random.uniform(splits[12], (DI,), jnp.float32) ** steps_of(splits[12], (DI,), ((0, 8),), -0.2, 0.2), 0.0, 2.0)
    proj_out = centred(splits[13], (DI, D), DI ** -0.5, 0.09375, ((0, 8),))
    expert_gate = centred(splits[14], (EXPERTS, FF, D), D ** -0.5, 0.09375, ((0, 2), (1, 16)))
    expert_up = centred(splits[15], (EXPERTS, FF, D), D ** -0.5, 0.09375, ((0, 2), (1, 16)))
    expert_down = centred(splits[16], (EXPERTS, FF, D), FF ** -0.5, 0.0625, ((0, 2), (1, 16)))
    expert_ids_keys = jax.random.split(jax.random.fold_in(splits[17], 1), STEPS * ROWS // ROW_DEV)
    expert_ids_turns = jax.random.permutation(jax.random.fold_in(splits[17], 3), STEPS * ROWS // ROW_DEV)
    expert_ids = jax.vmap(lambda own, number: routed_block(jax.random.fold_in(splits[17], 2), own, number, ROW_DEV, EXPERTS, TOP, CAP, 2))(expert_ids_keys, expert_ids_turns).reshape((STEPS, ROWS, TOP))
    route_weight = jnp.clip(0.2 + 0.8 * jax.random.uniform(splits[18], (STEPS, ROWS, TOP), jnp.float32) ** steps_of(splits[18], (STEPS, ROWS, TOP), ((1, 32),), -0.2, 0.2), 0.2, 1.0)
    return dict(layer_in=layer_in, conv_state=conv_state, ssm_state=ssm_state, proj_inner=proj_inner, proj_gate=proj_gate, conv_weight=conv_weight, conv_bias=conv_bias, delta_down=delta_down, state_proj=state_proj, delta_up=delta_up, delta_bias=delta_bias, decay_log=decay_log, skip_gain=skip_gain, proj_out=proj_out, expert_gate=expert_gate, expert_up=expert_up, expert_down=expert_down, expert_ids=expert_ids, route_weight=route_weight)


def rms_rows(values, eps):
    return values * lax.rsqrt(lax.optimization_barrier(jnp.mean(values * values, axis=-1, keepdims=True)) + eps)

def reference(layer_in, conv_state, ssm_state, proj_inner, proj_gate, conv_weight, conv_bias, delta_down, state_proj, delta_up, delta_bias, decay_log, skip_gain, proj_out, expert_gate, expert_up, expert_down, expert_ids, route_weight):
    slot_limit = N_DP * N_EXPERT * N_TENSOR * CAP
    flat_rows = jnp.arange(ROWS * TOP, dtype=jnp.int32) // TOP
    outputs = []
    for decode in range(STEPS):
        x_float = layer_in[decode].astype(jnp.float32)
        normed = rms_rows(x_float, 1e-06).astype(jnp.bfloat16)
        conv_input = jnp.dot(normed, proj_inner, preferred_element_type=jnp.float32).astype(jnp.bfloat16)
        gate_branch = jnp.dot(normed, proj_gate, preferred_element_type=jnp.float32)
        window = jnp.concatenate([conv_state, conv_input[:, None, :]], axis=1)
        conv_state = window[:, 1:, :]
        conv_sum = conv_bias + lax.optimization_barrier(jnp.sum(window.astype(jnp.float32) * conv_weight[None], axis=1))
        activated = jax.nn.silu(conv_sum).astype(jnp.bfloat16)
        delta_low = jnp.dot(activated, delta_down, preferred_element_type=jnp.float32)
        state_inputs = jnp.einsum('gc,knc->gkn', activated.astype(jnp.float32), state_proj.astype(jnp.float32))
        delta_normed = rms_rows(delta_low, 1e-06).astype(jnp.bfloat16)
        step_size = jax.nn.softplus(jnp.dot(delta_normed, delta_up, preferred_element_type=jnp.float32) + delta_bias)
        act_float = activated.astype(jnp.float32)
        decays = jnp.exp(-step_size[:, None, :] * jnp.exp(decay_log)[None])
        ssm_state = decays * ssm_state + step_size[:, None, :] * state_inputs[:, 0, :, None] * act_float[:, None, :]
        readout = lax.optimization_barrier(jnp.sum(ssm_state * state_inputs[:, 1, :, None], axis=1))
        gated_out = ((readout + skip_gain * act_float) * jax.nn.silu(gate_branch)).astype(jnp.bfloat16)
        residual = x_float + jnp.dot(gated_out, proj_out, preferred_element_type=jnp.float32)
        expert_in = rms_rows(residual, 1e-06).astype(jnp.bfloat16)
        flat_ids = expert_ids[decode].reshape(-1).astype(jnp.int32)
        flat_weight = route_weight[decode].reshape(-1)

        def one_expert(expert):
            mismatch = (flat_ids != expert).astype(jnp.int32)
            sorted_at = jnp.argsort(mismatch, stable=True)[:slot_limit]
            live_mask = (mismatch[sorted_at] == 0).astype(jnp.float32)
            row_index = flat_rows[sorted_at]
            selected = expert_in[row_index]
            gate_proj = jnp.dot(selected, expert_gate[expert].T, preferred_element_type=jnp.float32)
            up_proj = jnp.dot(selected, expert_up[expert].T, preferred_element_type=jnp.float32)
            activation = (jax.nn.silu(gate_proj) * up_proj).astype(jnp.bfloat16)
            expert_out = jnp.dot(activation, expert_down[expert], preferred_element_type=jnp.float32).astype(jnp.bfloat16)
            expert_out = lax.optimization_barrier(expert_out).astype(jnp.float32)
            return (expert_out * (flat_weight[sorted_at] * live_mask)[:, None], row_index)
        contribs, row_lists = lax.map(one_expert, jnp.arange(EXPERTS, dtype=jnp.int32))
        expert_sum = jnp.zeros((ROWS, D), jnp.float32).at[row_lists.reshape(-1)].add(contribs.reshape(-1, D))
        outputs.append((residual + expert_sum).astype(jnp.bfloat16))
    return (jnp.stack(outputs), conv_state, ssm_state)
```

```python
import functools

import jax
import jax.numpy as jnp
from jax import lax
from jax.experimental import pallas as pl
from jax.experimental.pallas import tpu as pltpu
from jax.sharding import PartitionSpec as P


BF = jnp.bfloat16
F32 = jnp.float32
PLANE = ("expert", "tensor")
NT = (((1,), (1,)), ((), ()))
VMEM_LIMIT = 48 << 20


def rms_rows(values, eps):
    return values * lax.rsqrt(jnp.mean(values * values, axis=-1, keepdims=True) + eps)


def swap(value, axes, size, mask):
    return lax.ppermute(value, axes, [(i, i ^ mask) for i in range(size)])


def gate_up_kernel(pieces, first, last, *refs):
    xs = refs[:pieces]
    refs = refs[pieces:]
    wg, wu = refs[:2]
    refs = refs[2:]
    if not first:
        g_in, u_in = refs[:2]
        refs = refs[2:]
    if last:
        w_ref = refs[0]
        refs = refs[1:]
    outs = refs[:-1]
    x = refs[-1]
    step = pl.program_id(0)
    rows = xs[0].shape[0]

    @pl.when(step == 0)
    def _():
        for i in range(pieces):
            x[i * rows : (i + 1) * rows, :] = xs[i][...]

    g = lax.dot_general(x[...], wg[...], NT, preferred_element_type=F32)
    u = lax.dot_general(x[...], wu[...], NT, preferred_element_type=F32)
    if not first:
        g = g + g_in[...]
        u = u + u_in[...]
    if last:
        blocks = pl.num_programs(0) // w_ref.shape[1]
        column = lax.broadcasted_iota(jnp.int32, w_ref.shape, 1)
        weight = jnp.sum(
            jnp.where(column == step // blocks, w_ref[...], 0.0), axis=1, keepdims=True
        )
        outs[0][...] = (g * jax.nn.sigmoid(g) * u * weight).astype(BF)
    else:
        outs[0][...] = g
        outs[1][...] = u


def gate_up(xs, wg, wu, chunk, chunks, partial, weights, block=256):
    hidden, width = wg.shape
    cols = width // chunks
    rows = xs[0].shape[0]
    total = rows * len(xs)
    first, last = partial is None, weights is not None
    x_spec = pl.BlockSpec((rows, cols), lambda i: (0, 0))
    w_spec = pl.BlockSpec((block, cols), lambda i: (i, chunk))
    h_spec = pl.BlockSpec((total, block), lambda i: (0, i))
    args = list(xs) + [wg, wu]
    specs = [x_spec] * len(xs) + [w_spec] * 2
    if not first:
        args += list(partial)
        specs += [h_spec] * 2
    if last:
        args.append(weights)
        specs.append(pl.BlockSpec(weights.shape, lambda i: (0, 0)))
        out_shape = [jax.ShapeDtypeStruct((total, hidden), BF)]
        out_specs = [h_spec]
    else:
        out_shape = [jax.ShapeDtypeStruct((total, hidden), F32)] * 2
        out_specs = [h_spec] * 2
    return pl.pallas_call(
        functools.partial(gate_up_kernel, len(xs), first, last),
        grid=(hidden // block,),
        in_specs=specs,
        out_specs=out_specs,
        out_shape=out_shape,
        scratch_shapes=[pltpu.VMEM((total, cols), BF)],
        compiler_params=pltpu.CompilerParams(
            vmem_limit_bytes=VMEM_LIMIT, dimension_semantics=("arbitrary",)
        ),
        cost_estimate=pl.CostEstimate(
            flops=4 * total * hidden * cols,
            bytes_accessed=4 * hidden * cols,
            transcendentals=0,
        ),
        name=f"gate_up_{chunk}",
    )(*args)


def down_kernel(a_ref, w_ref, own_ref, other_ref):
    y = jnp.dot(a_ref[...], w_ref[...], preferred_element_type=F32).astype(BF)
    half = own_ref.shape[0]
    own_ref[...] = y[:half]
    other_ref[...] = y[half:]


def down(act, wd, chunk, chunks, block=512):
    total, hidden = act.shape
    cols = wd.shape[1] // chunks
    offset = chunk * cols // block
    out = jax.ShapeDtypeStruct((total // 2, cols), BF)
    return pl.pallas_call(
        down_kernel,
        grid=(cols // block,),
        in_specs=[
            pl.BlockSpec((total, hidden), lambda i: (0, 0)),
            pl.BlockSpec((hidden, block), lambda i: (0, i + offset)),
        ],
        out_specs=[pl.BlockSpec((total // 2, block), lambda i: (0, i))] * 2,
        out_shape=[out] * 2,
        compiler_params=pltpu.CompilerParams(
            vmem_limit_bytes=VMEM_LIMIT, dimension_semantics=("arbitrary",)
        ),
        cost_estimate=pl.CostEstimate(
            flops=2 * total * hidden * cols, bytes_accessed=2 * hidden * cols, transcendentals=0
        ),
        name=f"down_{chunk}",
    )(act, wd)


def shards(
    layer_in,
    conv_state,
    ssm_state,
    proj_inner,
    proj_gate,
    conv_weight,
    conv_bias,
    delta_down,
    state_proj,
    delta_up,
    delta_bias,
    decay_log,
    skip_gain,
    proj_out,
    expert_gate,
    expert_up,
    expert_down,
    expert_ids,
    route_weight,
):
    steps, group_rows, width = layer_in.shape
    row_dev, top = expert_ids.shape[1:]
    planes = lax.axis_size("dp")
    group = lax.axis_size(PLANE)
    local_experts, hidden_dev = expert_gate.shape[:2]
    experts = local_experts * lax.axis_size("expert")
    place = lax.axis_index(PLANE)
    rank = delta_down.shape[1]
    taps = conv_weight.shape[0]
    n_state = decay_log.shape[0]
    chunks = 2

    x_float = layer_in.astype(F32)
    normed = rms_rows(x_float, 1e-06).astype(BF).reshape(steps * group_rows, width)
    conv_input = jnp.dot(normed, proj_inner, preferred_element_type=F32).astype(BF)
    conv_input = conv_input.reshape(steps, group_rows, -1)
    history = [conv_state[:, i] for i in range(taps - 1)] + [conv_input[s] for s in range(steps)]
    activated = []
    for s in range(steps):
        conv_sum = conv_bias + sum(
            history[s + k].astype(F32) * conv_weight[k][None] for k in range(taps)
        )
        activated.append(jax.nn.silu(conv_sum).astype(BF))
    conv_final = jnp.stack(history[steps:], axis=1)
    act_all = jnp.concatenate(activated, axis=0)
    sums = jnp.concatenate(
        [
            jnp.dot(act_all, delta_down, preferred_element_type=F32),
            lax.dot_general(
                act_all, state_proj.reshape(2 * n_state, -1), NT, preferred_element_type=F32
            ),
        ],
        axis=1,
    ).astype(BF)
    pair = (sums.astype(F32) + swap(sums, PLANE, group, 1).astype(F32)).astype(BF)
    total = pair.astype(F32)
    for mask in range(2, group, 2):
        total = total + swap(pair, PLANE, group, mask).astype(F32)
    gate_branch = jnp.dot(normed, proj_gate, preferred_element_type=F32)
    delta_normed = rms_rows(total[:, :rank], 1e-06).astype(BF)
    step_size = jax.nn.softplus(
        jnp.dot(delta_normed, delta_up, preferred_element_type=F32) + delta_bias
    ).reshape(steps, group_rows, -1)
    state_in = total[:, rank : rank + n_state].reshape(steps, group_rows, n_state)
    state_out = total[:, rank + n_state :].reshape(steps, group_rows, n_state)
    rate = jnp.exp(decay_log)
    gates = jax.nn.silu(gate_branch).reshape(steps, group_rows, -1)
    gated = []
    for s in range(steps):
        act_float = activated[s].astype(F32)
        decays = jnp.exp(-step_size[s][:, None, :] * rate[None])
        ssm_state = (
            decays * ssm_state
            + step_size[s][:, None, :] * state_in[s][:, :, None] * act_float[:, None, :]
        )
        readout = jnp.sum(ssm_state * state_out[s][:, :, None], axis=1)
        gated.append(((readout + skip_gain * act_float) * gates[s]).astype(BF))
    gated = jnp.concatenate(gated, axis=0)

    own = steps * row_dev
    row = lax.broadcasted_iota(jnp.int32, (group * own, steps * group_rows), 0)
    source = lax.broadcasted_iota(jnp.int32, (group * own, steps * group_rows), 1)
    device = jnp.bitwise_xor(row // own, place)
    wanted = (row % own) // row_dev * group_rows + device * row_dev + row % row_dev
    order = (source == wanted).astype(BF)
    gated = jnp.dot(order, gated, preferred_element_type=F32).astype(BF)
    gated = gated.reshape(group // 2, 2, own, -1)
    mix_other = jnp.dot(
        gated[:, 1].reshape(group // 2 * own, -1), proj_out, preferred_element_type=F32
    ).astype(BF)
    mix_own = jnp.dot(
        gated[:, 0].reshape(group // 2 * own, -1), proj_out, preferred_element_type=F32
    )
    pair = mix_own + swap(mix_other, PLANE, group, 1).astype(F32)
    mixer_out = pair[:own]
    for q in range(1, group // 2):
        block = pair[q * own : (q + 1) * own].astype(BF)
        mixer_out = mixer_out + swap(block, PLANE, group, 2 * q).astype(F32)
    own_rows = lax.dynamic_slice_in_dim(layer_in, place * row_dev, row_dev, 1)
    residual = own_rows.reshape(own, width).astype(F32) + mixer_out
    expert_in = rms_rows(residual, 1e-06).astype(BF)

    ids = expert_ids.reshape(own, top)
    table = jnp.sum(
        jnp.where(
            ids[:, :, None] == jnp.arange(experts, dtype=jnp.int32),
            route_weight.reshape(own, top)[:, :, None],
            0.0,
        ),
        axis=1,
    )
    high = table.astype(BF)
    low = (table - high.astype(F32)).astype(BF)
    extra = jnp.concatenate([high, low, jnp.zeros((own, 128 - 2 * experts), BF)], axis=1)

    cols = width // chunks
    partial = None
    act = None
    wg = expert_gate.reshape(local_experts * hidden_dev, width)
    wu = expert_up.reshape(local_experts * hidden_dev, width)
    wd = expert_down.reshape(local_experts * hidden_dev, width)
    for c in range(chunks):
        last = c == chunks - 1
        block = expert_in[:, c * cols : (c + 1) * cols]
        if last:
            block = jnp.concatenate([block, extra], axis=1)
        line = jnp.concatenate(
            [block] + [swap(block, "dp", planes, z) for z in range(1, planes)], axis=0
        )
        held = [line] + [swap(line, PLANE, group, 2 * q) for q in range(1, group // 2)]
        held = held + [swap(piece, PLANE, group, 1) for piece in held]
        weights = None
        if last:
            routed = jnp.concatenate([piece[:, cols:] for piece in held], axis=0).astype(F32)
            routed = routed[:, :experts] + routed[:, experts : 2 * experts]
            weights = lax.dynamic_slice_in_dim(
                routed, lax.axis_index("expert") * local_experts, local_experts, 1
            )
            held = [piece[:, :cols] for piece in held]
        partial = gate_up(held, wg, wu, c, chunks, partial, weights)
    act = partial[0]

    line_rows = planes * own
    outputs = []
    for c in range(chunks):
        mine, other = down(act, wd, c, chunks)
        pair = mine.astype(F32) + swap(other, PLANE, group, 1).astype(F32)
        line = pair[:line_rows]
        for q in range(1, group // 2):
            block = pair[q * line_rows : (q + 1) * line_rows].astype(BF)
            line = line + swap(block, PLANE, group, 2 * q).astype(F32)
        rows = residual[:, c * cols : (c + 1) * cols] + line[:own]
        for z in range(1, planes):
            block = line[z * own : (z + 1) * own].astype(BF)
            rows = rows + swap(block, "dp", planes, z).astype(F32)
        outputs.append(rows.astype(BF))
    layer_out = jnp.concatenate(outputs, axis=1).reshape(steps, row_dev, width)
    return (layer_out, conv_final, ssm_state)


def solution(mesh):
    placed = (
        P(None, "dp", None),
        P("dp", None, PLANE),
        P("dp", None, PLANE),
        P(None, PLANE),
        P(None, PLANE),
        P(None, PLANE),
        P(PLANE),
        P(PLANE, None),
        P(None, None, PLANE),
        P(None, PLANE),
        P(PLANE),
        P(None, PLANE),
        P(PLANE),
        P(PLANE, None),
        P("expert", ("dp", "tensor"), None),
        P("expert", ("dp", "tensor"), None),
        P("expert", ("dp", "tensor"), None),
        P(None, ("dp", "expert", "tensor"), None),
        P(None, ("dp", "expert", "tensor"), None),
    )
    return jax.shard_map(
        shards,
        mesh=mesh,
        in_specs=placed,
        out_specs=(
            P(None, ("dp", "expert", "tensor"), None),
            P("dp", None, PLANE),
            P("dp", None, PLANE),
        ),
        check_vma=False,
    )
```

```python
import functools

import jax
import jax.numpy as jnp
from jax import lax
from jax.experimental import pallas as pl
from jax.experimental.pallas import tpu as pltpu
from jax.sharding import PartitionSpec as P


BF = jnp.bfloat16
F32 = jnp.float32
PLANE = ("expert", "tensor")
NT = (((1,), (1,)), ((), ()))
VMEM_LIMIT = 48 << 20
HEAD_LIMIT = 16 << 20


def rms_rows(values, eps):
    return values * lax.rsqrt(jnp.mean(values * values, axis=-1, keepdims=True) + eps)


def swap(value, axes, size, mask):
    return lax.ppermute(value, axes, [(i, i ^ mask) for i in range(size)])


def head_kernel(
    steps, taps, n_state, x_ref, w_ref, state_ref, cw_ref, cb_ref, dd_ref, sp_ref,
    sums_ref, act_ref, conv_ref, scale_ref, acc, square,
):
    k = pl.program_id(0)
    x = x_ref[...].reshape(acc.shape[0], x_ref.shape[2])
    x_float = x.astype(F32)
    part = jnp.dot(x, w_ref[...], preferred_element_type=F32)
    squares = jnp.sum(x_float * x_float, axis=1, keepdims=True)

    @pl.when(k == 0)
    def _():
        acc[...] = part
        square[...] = squares

    @pl.when(k > 0)
    def _():
        acc[...] += part
        square[...] += squares

    @pl.when(k == pl.num_programs(0) - 1)
    def _():
        width = x_ref.shape[2] * pl.num_programs(0)
        scale = lax.rsqrt(square[...] / width + 1e-06)
        scale_ref[...] = scale
        conv_input = (acc[...] * scale).astype(BF)
        rows = acc.shape[0] // steps
        history = [state_ref[i] for i in range(taps - 1)]
        history += [conv_input[s * rows : (s + 1) * rows] for s in range(steps)]
        for i in range(taps - 1):
            conv_ref[i] = history[steps + i]
        for s in range(steps):
            total = cb_ref[...] + sum(
                history[s + i].astype(F32) * cw_ref[i : i + 1, :] for i in range(taps)
            )
            act_ref[s * rows : (s + 1) * rows, :] = (total * jax.nn.sigmoid(total)).astype(BF)
        act = act_ref[...]
        rank = dd_ref.shape[1]
        sums_ref[:, :rank] = jnp.dot(act, dd_ref[...], preferred_element_type=F32).astype(BF)
        sums_ref[:, rank:] = lax.dot_general(
            act, sp_ref[...], NT, preferred_element_type=F32
        ).astype(BF)


def head(layer_in, proj_inner, conv_state, conv_weight, conv_bias, delta_down, state_proj, block):
    steps, group_rows, width = layer_in.shape
    rows = steps * group_rows
    channels = proj_inner.shape[1]
    taps = conv_weight.shape[0]
    rank = delta_down.shape[1]
    n_sums = state_proj.shape[0]

    def whole(array):
        return pl.BlockSpec(array.shape, lambda k: (0,) * array.ndim)

    outs = [
        jax.ShapeDtypeStruct((rows, rank + n_sums), BF),
        jax.ShapeDtypeStruct((rows, channels), BF),
        jax.ShapeDtypeStruct(conv_state.shape, BF),
        jax.ShapeDtypeStruct((rows, 1), F32),
    ]
    rest = [conv_state, conv_weight, conv_bias, delta_down, state_proj]
    args = [
        pltpu.with_memory_space_constraint(array, pltpu.HBM)
        for array in [layer_in, proj_inner] + rest
    ]
    return pl.pallas_call(
        functools.partial(head_kernel, steps, taps, n_sums // 2),
        grid=(width // block,),
        in_specs=[
            pl.BlockSpec((steps, group_rows, block), lambda k: (0, 0, k)),
            pl.BlockSpec((block, channels), lambda k: (k, 0)),
        ]
        + [whole(array) for array in rest],
        out_specs=[whole(array) for array in outs],
        out_shape=outs,
        scratch_shapes=[pltpu.VMEM((rows, channels), F32), pltpu.VMEM((rows, 1), F32)],
        compiler_params=pltpu.CompilerParams(
            vmem_limit_bytes=HEAD_LIMIT, dimension_semantics=("arbitrary",)
        ),
        name="head",
    )(*args)


def mix_kernel(a_ref, w_ref, other_ref, own_ref):
    half = other_ref.shape[0]
    y = jnp.dot(a_ref[...], w_ref[...], preferred_element_type=F32)
    other_ref[...] = y[:half].astype(BF)
    own_ref[...] = y[half:]


def mix(a, w):
    rows, depth = a.shape
    cols = w.shape[1]
    return pl.pallas_call(
        mix_kernel,
        out_shape=[
            jax.ShapeDtypeStruct((rows // 2, cols), BF),
            jax.ShapeDtypeStruct((rows // 2, cols), F32),
        ],
        compiler_params=pltpu.CompilerParams(vmem_limit_bytes=16 << 20),
        cost_estimate=pl.CostEstimate(
            flops=2 * rows * depth * cols, bytes_accessed=2 * depth * cols, transcendentals=0
        ),
        name="mix",
    )(a, w)


def experts_kernel(
    pieces, chunks, experts, local_experts, block, cols, first_ref, *refs
):
    held = refs[:pieces]
    wg, wu, wd = refs[pieces : pieces + 3]
    outs = refs[pieces + 3 : pieces + 3 + 2 * chunks]
    x, tail, act, ring, down_ring, sems, down_sems = refs[pieces + 3 + 2 * chunks :]
    hidden, width = wg.shape
    rows = held[0].shape[0]
    slots, down_slots = ring.shape[0], down_ring.shape[0]
    up_steps, down_steps = hidden // block, width // cols

    def fetch(i, j):
        slot = lax.rem(i, slots)
        source = (wg, wu)[j]
        return pltpu.make_async_copy(
            source.at[pl.ds(i * block, block), :], ring.at[slot, j], sems.at[slot, j]
        )

    def fetch_down(i):
        slot = lax.rem(i, down_slots)
        return pltpu.make_async_copy(
            wd.at[:, pl.ds(i * cols, cols)], down_ring.at[slot], down_sems.at[slot]
        )

    for i in range(min(slots, up_steps)):
        fetch(i, 0).start()
        fetch(i, 1).start()
    for i in range(pieces):
        x[i * rows : (i + 1) * rows, :] = held[i][:, :width]
        tail[i * rows : (i + 1) * rows, :] = held[i][:, width:].astype(F32)
    lane = lax.broadcasted_iota(jnp.int32, tail.shape, 1)
    per_expert = up_steps // local_experts

    def up_step(i, carry):
        slot = lax.rem(i, slots)
        fetch(i, 0).wait()
        g = lax.dot_general(x[...], ring[slot, 0], NT, preferred_element_type=F32)
        fetch(i, 1).wait()
        u = lax.dot_general(x[...], ring[slot, 1], NT, preferred_element_type=F32)
        expert = first_ref[0] + i // per_expert
        chosen = (lane == expert) | (lane == expert + experts)
        weight = jnp.sum(jnp.where(chosen, tail[...], 0.0), axis=1, keepdims=True)
        act[:, pl.ds(pl.multiple_of(i * block, block), block)] = (
            g * jax.nn.sigmoid(g) * u * weight
        ).astype(BF)

        @pl.when(i + slots < up_steps)
        def _():
            fetch(i + slots, 0).start()
            fetch(i + slots, 1).start()

        @pl.when((i + slots >= up_steps) & (i + slots - up_steps < down_slots))
        def _():
            fetch_down(i + slots - up_steps).start()

        return carry

    lax.fori_loop(0, up_steps, up_step, 0)
    for i in range(min(slots, up_steps), min(down_slots, down_steps)):
        fetch_down(i).start()
    half = rows * pieces // 2
    chunk_steps = down_steps // chunks
    for c in range(chunks):

        def down_step(i, carry):
            step = i + c * chunk_steps
            fetch_down(step).wait()
            y = jnp.dot(
                act[...], down_ring[lax.rem(step, down_slots)], preferred_element_type=F32
            ).astype(BF)
            where = pl.ds(pl.multiple_of(i * cols, cols), cols)
            outs[2 * c][:, where] = y[:half]
            outs[2 * c + 1][:, where] = y[half:]

            @pl.when(step + down_slots < down_steps)
            def _():
                fetch_down(step + down_slots).start()

            return carry

        lax.fori_loop(0, chunk_steps, down_step, 0)


def expert_outputs(held, first, wg, wu, wd, experts, local_experts, chunks):
    pieces, rows = len(held), held[0].shape[0]
    hidden, width = wg.shape
    total = pieces * rows
    block = hidden // local_experts
    while block > 512:
        block //= 2
    cols = min(512, width // chunks)
    slots, down_slots = 2, 4
    vmem = pl.BlockSpec(memory_space=pltpu.VMEM)
    hbm = pl.BlockSpec(memory_space=pl.ANY)
    return pl.pallas_call(
        functools.partial(
            experts_kernel, pieces, chunks, experts, local_experts, block, cols
        ),
        in_specs=[pl.BlockSpec(memory_space=pltpu.SMEM)] + [vmem] * pieces + [hbm] * 3,
        out_specs=[vmem] * (2 * chunks),
        out_shape=[jax.ShapeDtypeStruct((total // 2, width // chunks), BF)] * (2 * chunks),
        scratch_shapes=[
            pltpu.VMEM((total, width), BF),
            pltpu.VMEM((total, held[0].shape[1] - width), F32),
            pltpu.VMEM((total, hidden), BF),
            pltpu.VMEM((slots, 2, block, width), BF),
            pltpu.VMEM((down_slots, hidden, cols), BF),
            pltpu.SemaphoreType.DMA((slots, 2)),
            pltpu.SemaphoreType.DMA((down_slots,)),
        ],
        compiler_params=pltpu.CompilerParams(vmem_limit_bytes=VMEM_LIMIT),
        cost_estimate=pl.CostEstimate(
            flops=6 * total * hidden * width,
            bytes_accessed=6 * hidden * width,
            transcendentals=total * hidden,
        ),
        name="experts",
    )(first, *held, wg, wu, wd)


def shards(
    layer_in,
    conv_state,
    ssm_state,
    proj_inner,
    proj_gate,
    conv_weight,
    conv_bias,
    delta_down,
    state_proj,
    delta_up,
    delta_bias,
    decay_log,
    skip_gain,
    proj_out,
    expert_gate,
    expert_up,
    expert_down,
    expert_ids,
    route_weight,
):
    steps, group_rows, width = layer_in.shape
    row_dev, top = expert_ids.shape[1:]
    planes = lax.axis_size("dp")
    group = lax.axis_size(PLANE)
    local_experts, hidden_dev = expert_gate.shape[:2]
    experts = local_experts * lax.axis_size("expert")
    place = lax.axis_index(PLANE)
    rank = delta_down.shape[1]
    n_state = decay_log.shape[0]
    chunks = 2

    sums, act_all, conv_final, scale = head(
        layer_in,
        proj_inner,
        jnp.transpose(conv_state, (1, 0, 2)),
        conv_weight,
        conv_bias[None],
        delta_down,
        state_proj.reshape(2 * n_state, -1),
        width // 4,
    )
    conv_final = jnp.transpose(conv_final, (1, 0, 2))
    pair = (sums.astype(F32) + swap(sums, PLANE, group, 1).astype(F32)).astype(BF)
    layer_rows, pair = lax.optimization_barrier((layer_in.reshape(-1, width), pair))
    total = pair.astype(F32)
    for mask in range(2, group, 2):
        total = total + swap(pair, PLANE, group, mask).astype(F32)
    gate_branch = jnp.dot(layer_rows, proj_gate, preferred_element_type=F32) * scale
    delta_normed = rms_rows(total[:, :rank], 1e-06).astype(BF)
    step_size = jax.nn.softplus(
        jnp.dot(delta_normed, delta_up, preferred_element_type=F32) + delta_bias
    ).reshape(steps, group_rows, -1)
    state_in = total[:, rank : rank + n_state].reshape(steps, group_rows, n_state)
    state_out = total[:, rank + n_state :].reshape(steps, group_rows, n_state)
    rate = jnp.exp(decay_log)
    gates = jax.nn.silu(gate_branch).reshape(steps, group_rows, -1)
    gated = []
    for s in range(steps):
        act_float = act_all[s * group_rows : (s + 1) * group_rows].astype(F32)
        decays = jnp.exp(-step_size[s][:, None, :] * rate[None])
        ssm_state = (
            decays * ssm_state
            + step_size[s][:, None, :] * state_in[s][:, :, None] * act_float[:, None, :]
        )
        readout = jnp.sum(ssm_state * state_out[s][:, :, None], axis=1)
        gated.append(((readout + skip_gain * act_float) * gates[s]).astype(BF))
    gated = jnp.concatenate(gated, axis=0)

    own = steps * row_dev
    row = lax.broadcasted_iota(jnp.int32, (group * own, steps * group_rows), 0)
    source = lax.broadcasted_iota(jnp.int32, (group * own, steps * group_rows), 1)
    half = group // 2
    distance = 2 * (row // own % half) + (row // own < half).astype(jnp.int32)
    device = jnp.bitwise_xor(distance, place)
    wanted = (row % own) // row_dev * group_rows + device * row_dev + row % row_dev
    order = (source == wanted).astype(BF)
    gated = jnp.dot(order, gated, preferred_element_type=F32).astype(BF)
    mix_other, mix_own = mix(gated, proj_out)
    pair = mix_own + swap(mix_other, PLANE, group, 1).astype(F32)
    mixer_out = pair[:own]
    for q in range(1, group // 2):
        block = pair[q * own : (q + 1) * own].astype(BF)
        mixer_out = mixer_out + swap(block, PLANE, group, 2 * q).astype(F32)
    own_rows = lax.dynamic_slice_in_dim(layer_in, place * row_dev, row_dev, 1)
    residual = own_rows.reshape(own, width).astype(F32) + mixer_out
    expert_in = rms_rows(residual, 1e-06).astype(BF)

    ids = expert_ids.reshape(own, top)
    table = jnp.sum(
        jnp.where(
            ids[:, :, None] == jnp.arange(experts, dtype=jnp.int32),
            route_weight.reshape(own, top)[:, :, None],
            0.0,
        ),
        axis=1,
    )
    high = table.astype(BF)
    low = (table - high.astype(F32)).astype(BF)
    extra = jnp.concatenate([high, low, jnp.zeros((own, 128 - 2 * experts), BF)], axis=1)

    block = jnp.concatenate([expert_in, extra], axis=1)
    line = jnp.concatenate(
        [block] + [swap(block, "dp", planes, z) for z in range(1, planes)], axis=0
    )
    held = [line] + [swap(line, PLANE, group, 2 * q) for q in range(1, group // 2)]
    held = held + [swap(piece, PLANE, group, 1) for piece in held]
    parts = expert_outputs(
        held,
        (lax.axis_index("expert") * local_experts)[None].astype(jnp.int32),
        expert_gate.reshape(local_experts * hidden_dev, width),
        expert_up.reshape(local_experts * hidden_dev, width),
        expert_down.reshape(local_experts * hidden_dev, width),
        experts,
        local_experts,
        chunks,
    )

    line_rows = planes * own
    lines = []
    for c in range(chunks):
        mine, other = parts[2 * c : 2 * c + 2]
        pair = mine.astype(F32) + swap(other, PLANE, group, 1).astype(F32)
        line = pair[:line_rows]
        for q in range(1, group // 2):
            block = pair[q * line_rows : (q + 1) * line_rows].astype(BF)
            line = line + swap(block, PLANE, group, 2 * q).astype(F32)
        lines.append(line)
    line = jnp.concatenate(lines, axis=1)
    rows = residual + line[:own]
    for z in range(1, planes):
        block = line[z * own : (z + 1) * own].astype(BF)
        rows = rows + swap(block, "dp", planes, z).astype(F32)
    layer_out = rows.astype(BF).reshape(steps, row_dev, width)
    return (layer_out, conv_final, ssm_state)


def solution(mesh):
    placed = (
        P(None, "dp", None),
        P("dp", None, PLANE),
        P("dp", None, PLANE),
        P(None, PLANE),
        P(None, PLANE),
        P(None, PLANE),
        P(PLANE),
        P(PLANE, None),
        P(None, None, PLANE),
        P(None, PLANE),
        P(PLANE),
        P(None, PLANE),
        P(PLANE),
        P(PLANE, None),
        P("expert", ("dp", "tensor"), None),
        P("expert", ("dp", "tensor"), None),
        P("expert", ("dp", "tensor"), None),
        P(None, ("dp", "expert", "tensor"), None),
        P(None, ("dp", "expert", "tensor"), None),
    )
    return jax.shard_map(
        shards,
        mesh=mesh,
        in_specs=placed,
        out_specs=(
            P(None, ("dp", "expert", "tensor"), None),
            P("dp", None, PLANE),
            P("dp", None, PLANE),
        ),
        check_vma=False,
    )
```

```python
import functools

import jax
import jax.numpy as jnp
from jax import lax
from jax.experimental import pallas as pl
from jax.experimental.pallas import tpu as pltpu
from jax.sharding import PartitionSpec as P


BF = jnp.bfloat16
F32 = jnp.float32
PLANE = ("expert", "tensor")
NT = (((1,), (1,)), ((), ()))
EXPERTS_LIMIT = 28 << 20
PRELOAD_LIMIT = 4 << 20
DOWN_LIMIT = 8 << 20
HEAD_LIMIT = 16 << 20


def rms_rows(values, eps):
    return values * lax.rsqrt(jnp.mean(values * values, axis=-1, keepdims=True) + eps)


def swap(value, axes, size, mask):
    return lax.ppermute(value, axes, [(i, i ^ mask) for i in range(size)])


def head_kernel(
    steps, taps, n_state, x_ref, w_ref, state_ref, cw_ref, cb_ref, dd_ref, sp_ref,
    sums_ref, act_ref, conv_ref, scale_ref, acc, square,
):
    k = pl.program_id(0)
    x = x_ref[...].reshape(acc.shape[0], x_ref.shape[2])
    x_float = x.astype(F32)
    part = jnp.dot(x, w_ref[...], preferred_element_type=F32)
    squares = jnp.sum(x_float * x_float, axis=1, keepdims=True)

    @pl.when(k == 0)
    def _():
        acc[...] = part
        square[...] = squares

    @pl.when(k > 0)
    def _():
        acc[...] += part
        square[...] += squares

    @pl.when(k == pl.num_programs(0) - 1)
    def _():
        width = x_ref.shape[2] * pl.num_programs(0)
        scale = lax.rsqrt(square[...] / width + 1e-06)
        scale_ref[...] = scale
        conv_input = (acc[...] * scale).astype(BF)
        rows = acc.shape[0] // steps
        history = [state_ref[i] for i in range(taps - 1)]
        history += [conv_input[s * rows : (s + 1) * rows] for s in range(steps)]
        for i in range(taps - 1):
            conv_ref[i] = history[steps + i]
        for s in range(steps):
            total = cb_ref[...] + sum(
                history[s + i].astype(F32) * cw_ref[i : i + 1, :] for i in range(taps)
            )
            act_ref[s * rows : (s + 1) * rows, :] = (total * jax.nn.sigmoid(total)).astype(BF)
        act = act_ref[...]
        rank = dd_ref.shape[1]
        sums_ref[:, :rank] = jnp.dot(act, dd_ref[...], preferred_element_type=F32).astype(BF)
        sums_ref[:, rank:] = lax.dot_general(
            act, sp_ref[...], NT, preferred_element_type=F32
        ).astype(BF)


def head(layer_in, proj_inner, conv_state, conv_weight, conv_bias, delta_down, state_proj, block):
    steps, group_rows, width = layer_in.shape
    rows = steps * group_rows
    channels = proj_inner.shape[1]
    taps = conv_weight.shape[0]
    rank = delta_down.shape[1]
    n_sums = state_proj.shape[0]

    def whole(array):
        return pl.BlockSpec(array.shape, lambda k: (0,) * array.ndim)

    outs = [
        jax.ShapeDtypeStruct((rows, rank + n_sums), BF),
        jax.ShapeDtypeStruct((rows, channels), BF),
        jax.ShapeDtypeStruct(conv_state.shape, BF),
        jax.ShapeDtypeStruct((rows, 1), F32),
    ]
    rest = [conv_state, conv_weight, conv_bias, delta_down, state_proj]
    args = [
        pltpu.with_memory_space_constraint(array, pltpu.HBM)
        for array in [layer_in, proj_inner] + rest
    ]
    return pl.pallas_call(
        functools.partial(head_kernel, steps, taps, n_sums // 2),
        grid=(width // block,),
        in_specs=[
            pl.BlockSpec((steps, group_rows, block), lambda k: (0, 0, k)),
            pl.BlockSpec((block, channels), lambda k: (k, 0)),
        ]
        + [whole(array) for array in rest],
        out_specs=[whole(array) for array in outs],
        out_shape=outs,
        scratch_shapes=[pltpu.VMEM((rows, channels), F32), pltpu.VMEM((rows, 1), F32)],
        compiler_params=pltpu.CompilerParams(
            vmem_limit_bytes=HEAD_LIMIT, dimension_semantics=("arbitrary",)
        ),
        name="head",
    )(*args)


def mix_kernel(a_ref, w_ref, other_ref, own_ref):
    half = other_ref.shape[0]
    y = jnp.dot(a_ref[...], w_ref[...], preferred_element_type=F32)
    other_ref[...] = y[:half].astype(BF)
    own_ref[...] = y[half:]


def mix(a, w):
    rows, depth = a.shape
    cols = w.shape[1]
    return pl.pallas_call(
        mix_kernel,
        out_shape=[
            jax.ShapeDtypeStruct((rows // 2, cols), BF),
            jax.ShapeDtypeStruct((rows // 2, cols), F32),
        ],
        compiler_params=pltpu.CompilerParams(vmem_limit_bytes=16 << 20),
        cost_estimate=pl.CostEstimate(
            flops=2 * rows * depth * cols, bytes_accessed=2 * depth * cols, transcendentals=0
        ),
        name="mix",
    )(a, w)


def preload_kernel(block, wg, wu, wd, g0, u0, down_ref, sems):
    copies = [
        pltpu.make_async_copy(wg.at[pl.ds(0, block), :], g0, sems.at[0]),
        pltpu.make_async_copy(wu.at[pl.ds(0, block), :], u0, sems.at[1]),
        pltpu.make_async_copy(wd, down_ref, sems.at[2]),
    ]
    for copy in copies:
        copy.start()
    for copy in copies:
        copy.wait()


def preload(wg, wu, wd, block):
    vmem = pl.BlockSpec(memory_space=pltpu.VMEM)
    hbm = pl.BlockSpec(memory_space=pl.ANY)
    width = wg.shape[1]
    return pl.pallas_call(
        functools.partial(preload_kernel, block),
        in_specs=[hbm] * 3,
        out_specs=[vmem] * 3,
        out_shape=[jax.ShapeDtypeStruct((block, width), BF)] * 2
        + [jax.ShapeDtypeStruct(wd.shape, BF)],
        scratch_shapes=[pltpu.SemaphoreType.DMA((3,))],
        compiler_params=pltpu.CompilerParams(vmem_limit_bytes=PRELOAD_LIMIT),
        cost_estimate=pl.CostEstimate(
            flops=0, bytes_accessed=4 * (2 * block * width + wd.size), transcendentals=0
        ),
        name="preload",
    )(wg, wu, wd)


def experts_kernel(pieces, experts, local_experts, block, first_ref, *refs):
    held = refs[:pieces]
    g0, u0, wg, wu, act = refs[pieces : pieces + 5]
    x, tail, ring, sems = refs[pieces + 5 :]
    hidden, width = wg.shape
    rows = held[0].shape[0]
    slots = ring.shape[0]
    up_steps = hidden // block

    def fetch(i, j):
        slot = lax.rem(i, slots)
        source = (wg, wu)[j]
        return pltpu.make_async_copy(
            source.at[pl.ds(i * block, block), :], ring.at[slot, j], sems.at[slot, j]
        )

    for i in range(1, min(slots + 1, up_steps)):
        fetch(i, 0).start()
        fetch(i, 1).start()
    for i in range(pieces):
        x[i * rows : (i + 1) * rows, :] = held[i][:, :width]
        tail[i * rows : (i + 1) * rows, :] = held[i][:, width:].astype(F32)
    lane = lax.broadcasted_iota(jnp.int32, tail.shape, 1)
    per_expert = up_steps // local_experts

    def activate(i, g, u):
        expert = first_ref[0] + i // per_expert
        chosen = (lane == expert) | (lane == expert + experts)
        weight = jnp.sum(jnp.where(chosen, tail[...], 0.0), axis=1, keepdims=True)
        return (g * jax.nn.sigmoid(g) * u * weight).astype(BF)

    g = lax.dot_general(x[...], g0[...], NT, preferred_element_type=F32)
    u = lax.dot_general(x[...], u0[...], NT, preferred_element_type=F32)
    act[:, :block] = activate(0, g, u)

    def up_step(i, carry):
        slot = lax.rem(i, slots)
        fetch(i, 0).wait()
        g = lax.dot_general(x[...], ring[slot, 0], NT, preferred_element_type=F32)
        fetch(i, 1).wait()
        u = lax.dot_general(x[...], ring[slot, 1], NT, preferred_element_type=F32)
        act[:, pl.ds(pl.multiple_of(i * block, block), block)] = activate(i, g, u)

        @pl.when(i + slots < up_steps)
        def _():
            fetch(i + slots, 0).start()
            fetch(i + slots, 1).start()

        return carry

    lax.fori_loop(1, up_steps, up_step, 0)


def down_kernel(offset, cols, act, wd, own_ref, other_ref):
    half = own_ref.shape[0]

    def step(i, carry):
        here = pl.ds(pl.multiple_of(i * cols, cols), cols)
        there = pl.ds(pl.multiple_of(offset + i * cols, cols), cols)
        y = jnp.dot(act[...], wd[:, there], preferred_element_type=F32).astype(BF)
        own_ref[:, here] = y[:half]
        other_ref[:, here] = y[half:]
        return carry

    lax.fori_loop(0, own_ref.shape[1] // cols, step, 0)


def up_block(hidden, local_experts):
    block = hidden // local_experts
    while block > 512:
        block //= 2
    return block


def expert_outputs(held, first, ready, wg, wu, experts, local_experts, chunks):
    pieces, rows = len(held), held[0].shape[0]
    hidden, width = wg.shape
    total = pieces * rows
    block = up_block(hidden, local_experts)
    cols = 512
    slots = 2
    vmem = pl.BlockSpec(memory_space=pltpu.VMEM)
    hbm = pl.BlockSpec(memory_space=pl.ANY)
    g0, u0, wd = ready
    act = pl.pallas_call(
        functools.partial(experts_kernel, pieces, experts, local_experts, block),
        in_specs=[pl.BlockSpec(memory_space=pltpu.SMEM)] + [vmem] * (pieces + 2) + [hbm] * 2,
        out_specs=vmem,
        out_shape=jax.ShapeDtypeStruct((total, hidden), BF),
        scratch_shapes=[
            pltpu.VMEM((total, width), BF),
            pltpu.VMEM((total, held[0].shape[1] - width), F32),
            pltpu.VMEM((slots, 2, block, width), BF),
            pltpu.SemaphoreType.DMA((slots, 2)),
        ],
        compiler_params=pltpu.CompilerParams(vmem_limit_bytes=EXPERTS_LIMIT),
        cost_estimate=pl.CostEstimate(
            flops=4 * total * hidden * width,
            bytes_accessed=4 * hidden * width,
            transcendentals=total * hidden,
        ),
        name="experts",
    )(first, *held, g0, u0, wg, wu)
    outs = []
    part = width // chunks
    for c in range(chunks):
        outs += pl.pallas_call(
            functools.partial(down_kernel, c * part, cols),
            in_specs=[vmem] * 2,
            out_specs=[vmem] * 2,
            out_shape=[jax.ShapeDtypeStruct((total // 2, part), BF)] * 2,
            compiler_params=pltpu.CompilerParams(vmem_limit_bytes=DOWN_LIMIT),
            cost_estimate=pl.CostEstimate(
                flops=2 * total * hidden * part,
                bytes_accessed=2 * hidden * part,
                transcendentals=0,
            ),
            name=f"down_{c}",
        )(act, wd)
    return outs


def shards(
    layer_in,
    conv_state,
    ssm_state,
    proj_inner,
    proj_gate,
    conv_weight,
    conv_bias,
    delta_down,
    state_proj,
    delta_up,
    delta_bias,
    decay_log,
    skip_gain,
    proj_out,
    expert_gate,
    expert_up,
    expert_down,
    expert_ids,
    route_weight,
):
    steps, group_rows, width = layer_in.shape
    row_dev, top = expert_ids.shape[1:]
    planes = lax.axis_size("dp")
    group = lax.axis_size(PLANE)
    local_experts, hidden_dev = expert_gate.shape[:2]
    experts = local_experts * lax.axis_size("expert")
    place = lax.axis_index(PLANE)
    rank = delta_down.shape[1]
    n_state = decay_log.shape[0]
    chunks = 2

    sums, act_all, conv_final, scale = head(
        layer_in,
        proj_inner,
        jnp.transpose(conv_state, (1, 0, 2)),
        conv_weight,
        conv_bias[None],
        delta_down,
        state_proj.reshape(2 * n_state, -1),
        width // 4,
    )
    conv_final = jnp.transpose(conv_final, (1, 0, 2))
    pair = (sums.astype(F32) + swap(sums, PLANE, group, 1).astype(F32)).astype(BF)
    layer_rows, pair = lax.optimization_barrier((layer_in.reshape(-1, width), pair))
    total = pair.astype(F32)
    for mask in range(2, group, 2):
        total = total + swap(pair, PLANE, group, mask).astype(F32)
    gate_branch = jnp.dot(layer_rows, proj_gate, preferred_element_type=F32) * scale
    delta_normed = rms_rows(total[:, :rank], 1e-06).astype(BF)
    step_size = jax.nn.softplus(
        jnp.dot(delta_normed, delta_up, preferred_element_type=F32) + delta_bias
    ).reshape(steps, group_rows, -1)
    state_in = total[:, rank : rank + n_state].reshape(steps, group_rows, n_state)
    state_out = total[:, rank + n_state :].reshape(steps, group_rows, n_state)
    rate = jnp.exp(decay_log)
    gates = jax.nn.silu(gate_branch).reshape(steps, group_rows, -1)
    gated = []
    for s in range(steps):
        act_float = act_all[s * group_rows : (s + 1) * group_rows].astype(F32)
        decays = jnp.exp(-step_size[s][:, None, :] * rate[None])
        ssm_state = (
            decays * ssm_state
            + step_size[s][:, None, :] * state_in[s][:, :, None] * act_float[:, None, :]
        )
        readout = jnp.sum(ssm_state * state_out[s][:, :, None], axis=1)
        gated.append(((readout + skip_gain * act_float) * gates[s]).astype(BF))
    gated = jnp.concatenate(gated, axis=0)

    own = steps * row_dev
    row = lax.broadcasted_iota(jnp.int32, (group * own, steps * group_rows), 0)
    source = lax.broadcasted_iota(jnp.int32, (group * own, steps * group_rows), 1)
    half = group // 2
    distance = 2 * (row // own % half) + (row // own < half).astype(jnp.int32)
    device = jnp.bitwise_xor(distance, place)
    wanted = (row % own) // row_dev * group_rows + device * row_dev + row % row_dev
    order = (source == wanted).astype(BF)
    gated = jnp.dot(order, gated, preferred_element_type=F32).astype(BF)
    mix_other, mix_own = mix(gated, proj_out)
    pair = mix_own + swap(mix_other, PLANE, group, 1).astype(F32)
    mixer_out = pair[:own]
    for q in range(1, group // 2):
        block = pair[q * own : (q + 1) * own].astype(BF)
        mixer_out = mixer_out + swap(block, PLANE, group, 2 * q).astype(F32)
    own_rows = lax.dynamic_slice_in_dim(layer_in, place * row_dev, row_dev, 1)
    residual = own_rows.reshape(own, width).astype(F32) + mixer_out
    expert_in = rms_rows(residual, 1e-06).astype(BF)

    ids = expert_ids.reshape(own, top)
    table = jnp.sum(
        jnp.where(
            ids[:, :, None] == jnp.arange(experts, dtype=jnp.int32),
            route_weight.reshape(own, top)[:, :, None],
            0.0,
        ),
        axis=1,
    )
    high = table.astype(BF)
    low = (table - high.astype(F32)).astype(BF)
    extra = jnp.concatenate([high, low, jnp.zeros((own, 128 - 2 * experts), BF)], axis=1)

    block = jnp.concatenate([expert_in, extra], axis=1)
    line = jnp.concatenate(
        [block] + [swap(block, "dp", planes, z) for z in range(1, planes)], axis=0
    )
    wg = expert_gate.reshape(local_experts * hidden_dev, width)
    wu = expert_up.reshape(local_experts * hidden_dev, width)
    wd = expert_down.reshape(local_experts * hidden_dev, width)
    line, wd = lax.optimization_barrier((line, wd))
    wg, wu, wd = [pltpu.with_memory_space_constraint(array, pltpu.HBM) for array in (wg, wu, wd)]
    ready = preload(wg, wu, wd, up_block(local_experts * hidden_dev, local_experts))
    held = [swap(line, PLANE, group, 2 * q) for q in range(1, group // 2)]
    held, ready = lax.optimization_barrier((held, ready))
    held = [line] + held
    held = held + [swap(piece, PLANE, group, 1) for piece in held]
    parts = expert_outputs(
        held,
        (lax.axis_index("expert") * local_experts)[None].astype(jnp.int32),
        ready,
        wg,
        wu,
        experts,
        local_experts,
        chunks,
    )

    line_rows = planes * own
    lines = []
    for c in range(chunks):
        mine, other = parts[2 * c : 2 * c + 2]
        pair = mine.astype(F32) + swap(other, PLANE, group, 1).astype(F32)
        line = pair[:line_rows]
        for q in range(1, group // 2):
            block = pair[q * line_rows : (q + 1) * line_rows].astype(BF)
            line = line + swap(block, PLANE, group, 2 * q).astype(F32)
        lines.append(line)
    line = jnp.concatenate(lines, axis=1)
    rows = residual + line[:own]
    for z in range(1, planes):
        block = line[z * own : (z + 1) * own].astype(BF)
        rows = rows + swap(block, "dp", planes, z).astype(F32)
    layer_out = rows.astype(BF).reshape(steps, row_dev, width)
    return (layer_out, conv_final, ssm_state)


def solution(mesh):
    placed = (
        P(None, "dp", None),
        P("dp", None, PLANE),
        P("dp", None, PLANE),
        P(None, PLANE),
        P(None, PLANE),
        P(None, PLANE),
        P(PLANE),
        P(PLANE, None),
        P(None, None, PLANE),
        P(None, PLANE),
        P(PLANE),
        P(None, PLANE),
        P(PLANE),
        P(PLANE, None),
        P("expert", ("dp", "tensor"), None),
        P("expert", ("dp", "tensor"), None),
        P("expert", ("dp", "tensor"), None),
        P(None, ("dp", "expert", "tensor"), None),
        P(None, ("dp", "expert", "tensor"), None),
    )
    return jax.shard_map(
        shards,
        mesh=mesh,
        in_specs=placed,
        out_specs=(
            P(None, ("dp", "expert", "tensor"), None),
            P("dp", None, PLANE),
            P("dp", None, PLANE),
        ),
        check_vma=False,
    )
```

```python
import functools

import jax
import jax.numpy as jnp
from jax import lax
from jax.experimental import pallas as pl
from jax.experimental.pallas import tpu as pltpu
from jax.sharding import PartitionSpec as P


BF = jnp.bfloat16
F32 = jnp.float32
PLANE = ("expert", "tensor")
NT = (((1,), (1,)), ((), ()))
EXPERTS_LIMIT = 28 << 20
PRELOAD_LIMIT = 4 << 20
DOWN_LIMIT = 8 << 20


def rms_rows(values, eps):
    return values * lax.rsqrt(jnp.mean(values * values, axis=-1, keepdims=True) + eps)


def swap(value, axes, size, mask):
    return lax.ppermute(value, axes, [(i, i ^ mask) for i in range(size)])


def head_kernel(
    steps, taps, parts,
    x_hbm, w_hbm, state_hbm, cw_hbm, cb_hbm, dd_hbm, sp_hbm,
    sums_ref, act_ref, conv_ref, scale_ref,
    x_ref, w_ref, state_ref, cw_ref, cb_ref, dd_ref, sp_ref, sems,
):
    group_rows, width = x_hbm.shape[1:]
    block = width // parts
    copies = [pltpu.make_async_copy(x_hbm, x_ref, sems.at[0])]
    for k in range(parts):
        rows = pl.ds(k * block, block)
        copies.append(pltpu.make_async_copy(w_hbm.at[rows], w_ref.at[rows], sems.at[1 + k]))
    rest = (
        (state_hbm, state_ref),
        (cw_hbm, cw_ref),
        (cb_hbm, cb_ref),
        (dd_hbm, dd_ref),
        (sp_hbm, sp_ref),
    )
    for i, (source, target) in enumerate(rest):
        copies.append(pltpu.make_async_copy(source, target, sems.at[1 + parts + i]))
    for copy in copies:
        copy.start()
    copies[0].wait()
    x = x_ref[...].reshape(steps * group_rows, width)
    x_float = x.astype(F32)
    scale = lax.rsqrt(jnp.mean(x_float * x_float, axis=1, keepdims=True) + 1e-06)
    scale_ref[...] = scale
    acc = None
    for k in range(parts):
        copies[1 + k].wait()
        part = jnp.dot(
            x[:, k * block : (k + 1) * block],
            w_ref[k * block : (k + 1) * block, :],
            preferred_element_type=F32,
        )
        acc = part if acc is None else acc + part
    conv_input = (acc * scale).astype(BF)
    for copy in copies[1 + parts :]:
        copy.wait()
    history = [state_ref[i] for i in range(taps - 1)]
    history += [conv_input[s * group_rows : (s + 1) * group_rows] for s in range(steps)]
    for i in range(taps - 1):
        conv_ref[i] = history[steps + i]
    for s in range(steps):
        total = cb_ref[...] + sum(
            history[s + i].astype(F32) * cw_ref[i : i + 1, :] for i in range(taps)
        )
        act_ref[s * group_rows : (s + 1) * group_rows, :] = (
            total * jax.nn.sigmoid(total)
        ).astype(BF)
    act = act_ref[...]
    rank = dd_ref.shape[1]
    sums_ref[:, :rank] = jnp.dot(act, dd_ref[...], preferred_element_type=F32).astype(BF)
    sums_ref[:, rank:] = lax.dot_general(
        act, sp_ref[...], NT, preferred_element_type=F32
    ).astype(BF)


def head(layer_in, proj_inner, conv_state, conv_weight, conv_bias, delta_down, state_proj):
    steps, group_rows, width = layer_in.shape
    rows = steps * group_rows
    channels = proj_inner.shape[1]
    rank = delta_down.shape[1]
    n_sums = state_proj.shape[0]
    parts = 4
    args = [layer_in, proj_inner, conv_state, conv_weight, conv_bias, delta_down, state_proj]
    outs = [
        jax.ShapeDtypeStruct((rows, rank + n_sums), BF),
        jax.ShapeDtypeStruct((rows, channels), BF),
        jax.ShapeDtypeStruct(conv_state.shape, BF),
        jax.ShapeDtypeStruct((rows, 1), F32),
    ]
    return pl.pallas_call(
        functools.partial(head_kernel, steps, conv_weight.shape[0], parts),
        in_specs=[pl.BlockSpec(memory_space=pl.ANY)] * len(args),
        out_specs=[pl.BlockSpec(memory_space=pltpu.VMEM)] * len(outs),
        out_shape=outs,
        scratch_shapes=[pltpu.VMEM(array.shape, array.dtype) for array in args]
        + [pltpu.SemaphoreType.DMA((parts + len(args) - 1,))],
        compiler_params=pltpu.CompilerParams(vmem_limit_bytes=16 << 20),
        name="head",
    )(*[pltpu.with_memory_space_constraint(array, pltpu.HBM) for array in args])


def finish_kernel(residual_ref, line_ref, *refs):
    out_ref = refs[-1]
    rows = residual_ref[...] + line_ref[...]
    for ref in refs[:-1]:
        rows = rows + ref[...].astype(F32)
    rows = rows.astype(BF)
    each = out_ref.shape[1]
    for s in range(out_ref.shape[0]):
        out_ref[s] = rows[s * each : (s + 1) * each]


def finish(residual, line, received, steps):
    rows, width = residual.shape
    return pl.pallas_call(
        finish_kernel,
        out_shape=jax.ShapeDtypeStruct((steps, rows // steps, width), BF),
        compiler_params=pltpu.CompilerParams(vmem_limit_bytes=4 << 20),
        name="finish",
    )(residual, line, *received)


def mixer_kernel(steps, n_state, received, *refs):
    sums = refs[: 1 + received]
    (
        act_ref, gate_ref, du_ref, db_ref, dl_ref, sg_ref, order_ref, st_ref, wo_ref,
        new_hbm, other_ref, own_ref, new_ref, read_ref, sem,
    ) = refs[1 + received :]
    total = sum(ref[...].astype(F32) for ref in sums)
    rank = du_ref.shape[0]
    low = total[:, :rank]
    scale = lax.rsqrt(jnp.mean(low * low, axis=1, keepdims=True) + 1e-06)
    raw = jnp.dot((low * scale).astype(BF), du_ref[...], preferred_element_type=F32) + db_ref[...]
    step_size = jnp.maximum(raw, 0.0) + jnp.log1p(jnp.exp(-jnp.abs(raw)))
    act = act_ref[...].astype(F32)
    rate = jnp.exp(dl_ref[...])
    rows = act.shape[0] // steps
    drive = step_size * act
    columns = total[:, rank:].T
    for r in range(rows):
        where = slice(r * n_state, (r + 1) * n_state)
        state = st_ref[where, :]
        for s in range(steps):
            i = s * rows + r
            decay = jnp.exp(-step_size[i : i + 1] * rate)
            state = decay * state + drive[i : i + 1] * columns[:n_state, i : i + 1]
            read_ref[i : i + 1, :] = jnp.sum(
                state * columns[n_state:, i : i + 1], axis=0, keepdims=True
            )
        new_ref[where, :] = state
    gated = ((read_ref[...] + sg_ref[...] * act) * gate_ref[...]).astype(BF)
    copy = pltpu.make_async_copy(new_ref, new_hbm, sem)
    copy.start()
    gated = jnp.dot(order_ref[...], gated, preferred_element_type=F32).astype(BF)
    y = jnp.dot(gated, wo_ref[...], preferred_element_type=F32)
    half = other_ref.shape[0]
    other_ref[...] = y[:half].astype(BF)
    own_ref[...] = y[half:]
    copy.wait()


def mixer(sums, act, gate, delta_up, delta_bias, decay_log, skip_gain, order, state, wo, steps):
    rows, channels = act.shape
    n_state = decay_log.shape[0]
    width = wo.shape[1]
    vmem = pl.BlockSpec(memory_space=pltpu.VMEM)
    args = list(sums)
    args += [act, gate, delta_up, delta_bias, decay_log, skip_gain, order, state, wo]
    return pl.pallas_call(
        functools.partial(mixer_kernel, steps, n_state, len(sums) - 1),
        in_specs=[vmem] * len(args),
        out_specs=[pl.BlockSpec(memory_space=pl.ANY), vmem, vmem],
        out_shape=[
            jax.ShapeDtypeStruct(state.shape, F32),
            jax.ShapeDtypeStruct((rows // 2, width), BF),
            jax.ShapeDtypeStruct((rows // 2, width), F32),
        ],
        scratch_shapes=[
            pltpu.VMEM(state.shape, F32),
            pltpu.VMEM((rows, channels), F32),
            pltpu.SemaphoreType.DMA,
        ],
        compiler_params=pltpu.CompilerParams(vmem_limit_bytes=16 << 20),
        cost_estimate=pl.CostEstimate(
            flops=2 * rows * channels * width,
            bytes_accessed=2 * channels * width,
            transcendentals=rows * n_state * channels,
        ),
        name="mixer",
    )(*args)


def preload_kernel(block, wg, wu, wd, g0, u0, down_ref, sems):
    copies = [
        pltpu.make_async_copy(wg.at[pl.ds(0, block), :], g0, sems.at[0]),
        pltpu.make_async_copy(wu.at[pl.ds(0, block), :], u0, sems.at[1]),
        pltpu.make_async_copy(wd, down_ref, sems.at[2]),
    ]
    for copy in copies:
        copy.start()
    for copy in copies:
        copy.wait()


def preload(wg, wu, wd, block):
    vmem = pl.BlockSpec(memory_space=pltpu.VMEM)
    hbm = pl.BlockSpec(memory_space=pl.ANY)
    width = wg.shape[1]
    return pl.pallas_call(
        functools.partial(preload_kernel, block),
        in_specs=[hbm] * 3,
        out_specs=[vmem] * 3,
        out_shape=[jax.ShapeDtypeStruct((block, width), BF)] * 2
        + [jax.ShapeDtypeStruct(wd.shape, BF)],
        scratch_shapes=[pltpu.SemaphoreType.DMA((3,))],
        compiler_params=pltpu.CompilerParams(vmem_limit_bytes=PRELOAD_LIMIT),
        cost_estimate=pl.CostEstimate(
            flops=0, bytes_accessed=4 * (2 * block * width + wd.size), transcendentals=0
        ),
        name="preload",
    )(wg, wu, wd)


def experts_kernel(pieces, experts, local_experts, block, first_ref, *refs):
    held = refs[:pieces]
    g0, u0, wg, wu, act = refs[pieces : pieces + 5]
    x, tail, ring, sems = refs[pieces + 5 :]
    hidden, width = wg.shape
    rows = held[0].shape[0]
    slots = ring.shape[0]
    up_steps = hidden // block

    def fetch(i, j):
        slot = lax.rem(i, slots)
        source = (wg, wu)[j]
        return pltpu.make_async_copy(
            source.at[pl.ds(i * block, block), :], ring.at[slot, j], sems.at[slot, j]
        )

    for i in range(1, min(slots + 1, up_steps)):
        fetch(i, 0).start()
        fetch(i, 1).start()
    for i in range(pieces):
        x[i * rows : (i + 1) * rows, :] = held[i][:, :width]
        tail[i * rows : (i + 1) * rows, :] = held[i][:, width:].astype(F32)
    lane = lax.broadcasted_iota(jnp.int32, tail.shape, 1)
    per_expert = up_steps // local_experts

    def activate(i, g, u):
        expert = first_ref[0] + i // per_expert
        chosen = (lane == expert) | (lane == expert + experts)
        weight = jnp.sum(jnp.where(chosen, tail[...], 0.0), axis=1, keepdims=True)
        return (g * jax.nn.sigmoid(g) * u * weight).astype(BF)

    g = lax.dot_general(x[...], g0[...], NT, preferred_element_type=F32)
    u = lax.dot_general(x[...], u0[...], NT, preferred_element_type=F32)
    act[:, :block] = activate(0, g, u)

    def up_step(i, carry):
        slot = lax.rem(i, slots)
        fetch(i, 0).wait()
        g = lax.dot_general(x[...], ring[slot, 0], NT, preferred_element_type=F32)
        fetch(i, 1).wait()
        u = lax.dot_general(x[...], ring[slot, 1], NT, preferred_element_type=F32)
        act[:, pl.ds(pl.multiple_of(i * block, block), block)] = activate(i, g, u)

        @pl.when(i + slots < up_steps)
        def _():
            fetch(i + slots, 0).start()
            fetch(i + slots, 1).start()

        return carry

    lax.fori_loop(1, up_steps, up_step, 0)


def down_kernel(offset, cols, act, wd, own_ref, other_ref):
    half = own_ref.shape[0]

    def step(i, carry):
        here = pl.ds(pl.multiple_of(i * cols, cols), cols)
        there = pl.ds(pl.multiple_of(offset + i * cols, cols), cols)
        y = jnp.dot(act[...], wd[:, there], preferred_element_type=F32).astype(BF)
        own_ref[:, here] = y[:half]
        other_ref[:, here] = y[half:]
        return carry

    lax.fori_loop(0, own_ref.shape[1] // cols, step, 0)


def up_block(hidden, local_experts):
    block = hidden // local_experts
    while block > 512:
        block //= 2
    return block


def expert_outputs(held, first, ready, wg, wu, experts, local_experts, chunks):
    pieces, rows = len(held), held[0].shape[0]
    hidden, width = wg.shape
    total = pieces * rows
    block = up_block(hidden, local_experts)
    cols = 512
    slots = 2
    vmem = pl.BlockSpec(memory_space=pltpu.VMEM)
    hbm = pl.BlockSpec(memory_space=pl.ANY)
    g0, u0, wd = ready
    act = pl.pallas_call(
        functools.partial(experts_kernel, pieces, experts, local_experts, block),
        in_specs=[pl.BlockSpec(memory_space=pltpu.SMEM)] + [vmem] * (pieces + 2) + [hbm] * 2,
        out_specs=vmem,
        out_shape=jax.ShapeDtypeStruct((total, hidden), BF),
        scratch_shapes=[
            pltpu.VMEM((total, width), BF),
            pltpu.VMEM((total, held[0].shape[1] - width), F32),
            pltpu.VMEM((slots, 2, block, width), BF),
            pltpu.SemaphoreType.DMA((slots, 2)),
        ],
        compiler_params=pltpu.CompilerParams(vmem_limit_bytes=EXPERTS_LIMIT),
        cost_estimate=pl.CostEstimate(
            flops=4 * total * hidden * width,
            bytes_accessed=4 * hidden * width,
            transcendentals=total * hidden,
        ),
        name="experts",
    )(first, *held, g0, u0, wg, wu)
    outs = []
    part = width // chunks
    for c in range(chunks):
        outs += pl.pallas_call(
            functools.partial(down_kernel, c * part, cols),
            in_specs=[vmem] * 2,
            out_specs=[vmem] * 2,
            out_shape=[jax.ShapeDtypeStruct((total // 2, part), BF)] * 2,
            compiler_params=pltpu.CompilerParams(vmem_limit_bytes=DOWN_LIMIT),
            cost_estimate=pl.CostEstimate(
                flops=2 * total * hidden * part,
                bytes_accessed=2 * hidden * part,
                transcendentals=0,
            ),
            name=f"down_{c}",
        )(act, wd)
    return outs


def shards(
    layer_in,
    conv_state,
    ssm_state,
    proj_inner,
    proj_gate,
    conv_weight,
    conv_bias,
    delta_down,
    state_proj,
    delta_up,
    delta_bias,
    decay_log,
    skip_gain,
    proj_out,
    expert_gate,
    expert_up,
    expert_down,
    expert_ids,
    route_weight,
):
    steps, group_rows, width = layer_in.shape
    row_dev, top = expert_ids.shape[1:]
    planes = lax.axis_size("dp")
    group = lax.axis_size(PLANE)
    local_experts, hidden_dev = expert_gate.shape[:2]
    experts = local_experts * lax.axis_size("expert")
    place = lax.axis_index(PLANE)
    rank = delta_down.shape[1]
    n_state = decay_log.shape[0]
    chunks = 2

    sums, act_all, conv_final, scale = head(
        layer_in,
        proj_inner,
        jnp.transpose(conv_state, (1, 0, 2)),
        conv_weight,
        conv_bias[None],
        delta_down,
        state_proj.reshape(2 * n_state, -1),
    )
    conv_final = jnp.transpose(conv_final, (1, 0, 2))
    pair = (sums.astype(F32) + swap(sums, PLANE, group, 1).astype(F32)).astype(BF)
    layer_rows, pair = lax.optimization_barrier((layer_in.reshape(-1, width), pair))
    sums = [pair] + [swap(pair, PLANE, group, mask) for mask in range(2, group, 2)]
    gate = jax.nn.silu(jnp.dot(layer_rows, proj_gate, preferred_element_type=F32) * scale)

    own = steps * row_dev
    row = lax.broadcasted_iota(jnp.int32, (group * own, steps * group_rows), 0)
    source = lax.broadcasted_iota(jnp.int32, (group * own, steps * group_rows), 1)
    half = group // 2
    distance = 2 * (row // own % half) + (row // own < half).astype(jnp.int32)
    device = jnp.bitwise_xor(distance, place)
    wanted = (row % own) // row_dev * group_rows + device * row_dev + row % row_dev
    order = (source == wanted).astype(BF)
    channels = proj_inner.shape[1]
    new_state, mix_other, mix_own = mixer(
        sums,
        act_all,
        gate,
        delta_up,
        delta_bias[None],
        decay_log,
        skip_gain[None],
        order,
        ssm_state.reshape(group_rows * n_state, channels),
        proj_out,
        steps,
    )
    ssm_state = new_state.reshape(ssm_state.shape)
    pair = mix_own + swap(mix_other, PLANE, group, 1).astype(F32)
    mixer_out = pair[:own]
    for q in range(1, group // 2):
        block = pair[q * own : (q + 1) * own].astype(BF)
        mixer_out = mixer_out + swap(block, PLANE, group, 2 * q).astype(F32)
    own_rows = lax.dynamic_slice_in_dim(layer_in, place * row_dev, row_dev, 1)
    residual = own_rows.reshape(own, width).astype(F32) + mixer_out
    expert_in = rms_rows(residual, 1e-06).astype(BF)

    ids = expert_ids.reshape(own, top)
    table = jnp.sum(
        jnp.where(
            ids[:, :, None] == jnp.arange(experts, dtype=jnp.int32),
            route_weight.reshape(own, top)[:, :, None],
            0.0,
        ),
        axis=1,
    )
    high = table.astype(BF)
    low = (table - high.astype(F32)).astype(BF)
    extra = jnp.concatenate([high, low, jnp.zeros((own, 128 - 2 * experts), BF)], axis=1)

    block = jnp.concatenate([expert_in, extra], axis=1)
    along = {z: swap(block, "dp", planes, z) for z in reversed(range(1, planes))}
    line = jnp.concatenate([block] + [along[z] for z in range(1, planes)], axis=0)
    wg = expert_gate.reshape(local_experts * hidden_dev, width)
    wu = expert_up.reshape(local_experts * hidden_dev, width)
    wd = expert_down.reshape(local_experts * hidden_dev, width)
    line, wd = lax.optimization_barrier((line, wd))
    wg, wu, wd = [pltpu.with_memory_space_constraint(array, pltpu.HBM) for array in (wg, wu, wd)]
    ready = preload(wg, wu, wd, up_block(local_experts * hidden_dev, local_experts))
    held = [swap(line, PLANE, group, 2 * q) for q in range(1, group // 2)]
    held, ready = lax.optimization_barrier((held, ready))
    held = [line] + held
    held = held + [swap(piece, PLANE, group, 1) for piece in held]
    parts = expert_outputs(
        held,
        (lax.axis_index("expert") * local_experts)[None].astype(jnp.int32),
        ready,
        wg,
        wu,
        experts,
        local_experts,
        chunks,
    )

    line_rows = planes * own
    lines = []
    for c in range(chunks):
        mine, other = parts[2 * c : 2 * c + 2]
        pair = mine.astype(F32) + swap(other, PLANE, group, 1).astype(F32)
        line = pair[:line_rows]
        for q in range(1, group // 2):
            block = pair[q * line_rows : (q + 1) * line_rows].astype(BF)
            line = line + swap(block, PLANE, group, 2 * q).astype(F32)
        lines.append(line)
    line = jnp.concatenate(lines, axis=1)
    received = []
    for z in range(1, planes):
        block = line[z * own : (z + 1) * own].astype(BF)
        received.append(swap(block, "dp", planes, z))
    layer_out = finish(residual, line[:own], received, steps)
    return (layer_out, conv_final, ssm_state)


def solution(mesh):
    placed = (
        P(None, "dp", None),
        P("dp", None, PLANE),
        P("dp", None, PLANE),
        P(None, PLANE),
        P(None, PLANE),
        P(None, PLANE),
        P(PLANE),
        P(PLANE, None),
        P(None, None, PLANE),
        P(None, PLANE),
        P(PLANE),
        P(None, PLANE),
        P(PLANE),
        P(PLANE, None),
        P("expert", ("dp", "tensor"), None),
        P("expert", ("dp", "tensor"), None),
        P("expert", ("dp", "tensor"), None),
        P(None, ("dp", "expert", "tensor"), None),
        P(None, ("dp", "expert", "tensor"), None),
    )
    return jax.shard_map(
        shards,
        mesh=mesh,
        in_specs=placed,
        out_specs=(
            P(None, ("dp", "expert", "tensor"), None),
            P("dp", None, PLANE),
            P("dp", None, PLANE),
        ),
        check_vma=False,
    )
```

```python
import functools

import jax
import jax.numpy as jnp
from jax import lax
from jax.experimental import pallas as pl
from jax.experimental.pallas import tpu as pltpu
from jax.sharding import PartitionSpec as P


BF = jnp.bfloat16
F32 = jnp.float32
PLANE = ("expert", "tensor")
NT = (((1,), (1,)), ((), ()))
EXPERTS_LIMIT = 28 << 20
PRELOAD_LIMIT = 4 << 20
DOWN_LIMIT = 8 << 20


def rms_rows(values, eps):
    return values * lax.rsqrt(jnp.mean(values * values, axis=-1, keepdims=True) + eps)


def swap(value, axes, size, mask):
    return lax.ppermute(value, axes, [(i, i ^ mask) for i in range(size)])


def head_kernel(
    steps, taps, parts,
    x_hbm, w_hbm, state_hbm, cw_hbm, cb_hbm, dd_hbm, sp_hbm,
    sums_ref, act_ref, conv_ref, scale_ref,
    x_ref, w_ref, state_ref, cw_ref, cb_ref, dd_ref, sp_ref, sems,
):
    group_rows, width = x_hbm.shape[1:]
    block = width // parts
    copies = [pltpu.make_async_copy(x_hbm, x_ref, sems.at[0])]
    for k in range(parts):
        rows = pl.ds(k * block, block)
        copies.append(pltpu.make_async_copy(w_hbm.at[rows], w_ref.at[rows], sems.at[1 + k]))
    rest = (
        (state_hbm, state_ref),
        (cw_hbm, cw_ref),
        (cb_hbm, cb_ref),
        (dd_hbm, dd_ref),
        (sp_hbm, sp_ref),
    )
    for i, (source, target) in enumerate(rest):
        copies.append(pltpu.make_async_copy(source, target, sems.at[1 + parts + i]))
    for copy in copies:
        copy.start()
    copies[0].wait()
    x = x_ref[...].reshape(steps * group_rows, width)
    x_float = x.astype(F32)
    scale = lax.rsqrt(jnp.mean(x_float * x_float, axis=1, keepdims=True) + 1e-06)
    scale_ref[...] = scale
    acc = None
    for k in range(parts):
        copies[1 + k].wait()
        part = jnp.dot(
            x[:, k * block : (k + 1) * block],
            w_ref[k * block : (k + 1) * block, :],
            preferred_element_type=F32,
        )
        acc = part if acc is None else acc + part
    conv_input = (acc * scale).astype(BF)
    for copy in copies[1 + parts :]:
        copy.wait()
    history = [state_ref[i] for i in range(taps - 1)]
    history += [conv_input[s * group_rows : (s + 1) * group_rows] for s in range(steps)]
    for i in range(taps - 1):
        conv_ref[i] = history[steps + i]
    for s in range(steps):
        total = cb_ref[...] + sum(
            history[s + i].astype(F32) * cw_ref[i : i + 1, :] for i in range(taps)
        )
        act_ref[s * group_rows : (s + 1) * group_rows, :] = (
            total * jax.nn.sigmoid(total)
        ).astype(BF)
    act = act_ref[...]
    rank = dd_ref.shape[1]
    sums_ref[:, :rank] = jnp.dot(act, dd_ref[...], preferred_element_type=F32).astype(BF)
    sums_ref[:, rank:] = lax.dot_general(
        act, sp_ref[...], NT, preferred_element_type=F32
    ).astype(BF)


def head(layer_in, proj_inner, conv_state, conv_weight, conv_bias, delta_down, state_proj):
    steps, group_rows, width = layer_in.shape
    rows = steps * group_rows
    channels = proj_inner.shape[1]
    rank = delta_down.shape[1]
    n_sums = state_proj.shape[0]
    parts = 4
    args = [layer_in, proj_inner, conv_state, conv_weight, conv_bias, delta_down, state_proj]
    outs = [
        jax.ShapeDtypeStruct((rows, rank + n_sums), BF),
        jax.ShapeDtypeStruct((rows, channels), BF),
        jax.ShapeDtypeStruct(conv_state.shape, BF),
        jax.ShapeDtypeStruct((rows, 1), F32),
    ]
    return pl.pallas_call(
        functools.partial(head_kernel, steps, conv_weight.shape[0], parts),
        in_specs=[pl.BlockSpec(memory_space=pl.ANY)] * len(args),
        out_specs=[pl.BlockSpec(memory_space=pltpu.VMEM)] * len(outs),
        out_shape=outs,
        scratch_shapes=[pltpu.VMEM(array.shape, array.dtype) for array in args]
        + [pltpu.SemaphoreType.DMA((parts + len(args) - 1,))],
        compiler_params=pltpu.CompilerParams(vmem_limit_bytes=16 << 20),
        name="head",
    )(*[pltpu.with_memory_space_constraint(array, pltpu.HBM) for array in args])


def finish_kernel(chunks, residual_ref, *refs):
    out_ref = refs[-1]
    each = out_ref.shape[1]
    per_chunk = (len(refs) - 1) // chunks
    for c in range(chunks):
        parts = refs[c * per_chunk : (c + 1) * per_chunk]
        cols = parts[0].shape[1]
        here = slice(c * cols, (c + 1) * cols)
        rows = residual_ref[:, here]
        for ref in parts:
            rows = rows + ref[...].astype(F32)
        rows = rows.astype(BF)
        for s in range(out_ref.shape[0]):
            out_ref[s, :, here] = rows[s * each : (s + 1) * each]


def finish(residual, chunks, steps):
    rows, width = residual.shape
    return pl.pallas_call(
        functools.partial(finish_kernel, len(chunks)),
        out_shape=jax.ShapeDtypeStruct((steps, rows // steps, width), BF),
        compiler_params=pltpu.CompilerParams(vmem_limit_bytes=4 << 20),
        name="finish",
    )(residual, *[value for chunk in chunks for value in chunk])


def mixer_kernel(steps, n_state, received, *refs):
    sums = refs[: 1 + received]
    (
        act_ref, gate_ref, du_ref, db_ref, dl_ref, sg_ref, order_ref, st_ref, wo_ref,
        new_hbm, other_ref, own_ref, new_ref, read_ref, sem,
    ) = refs[1 + received :]
    total = sum(ref[...].astype(F32) for ref in sums)
    rank = du_ref.shape[0]
    low = total[:, :rank]
    scale = lax.rsqrt(jnp.mean(low * low, axis=1, keepdims=True) + 1e-06)
    raw = jnp.dot((low * scale).astype(BF), du_ref[...], preferred_element_type=F32) + db_ref[...]
    step_size = jnp.maximum(raw, 0.0) + jnp.log1p(jnp.exp(-jnp.abs(raw)))
    act = act_ref[...].astype(F32)
    rate = jnp.exp(dl_ref[...])
    rows = act.shape[0] // steps
    drive = step_size * act
    columns = total[:, rank:].T
    for r in range(rows):
        where = slice(r * n_state, (r + 1) * n_state)
        state = st_ref[where, :]
        for s in range(steps):
            i = s * rows + r
            decay = jnp.exp(-step_size[i : i + 1] * rate)
            state = decay * state + drive[i : i + 1] * columns[:n_state, i : i + 1]
            read_ref[i : i + 1, :] = jnp.sum(
                state * columns[n_state:, i : i + 1], axis=0, keepdims=True
            )
        new_ref[where, :] = state
    gated = ((read_ref[...] + sg_ref[...] * act) * gate_ref[...]).astype(BF)
    copy = pltpu.make_async_copy(new_ref, new_hbm, sem)
    copy.start()
    gated = jnp.dot(order_ref[...], gated, preferred_element_type=F32).astype(BF)
    y = jnp.dot(gated, wo_ref[...], preferred_element_type=F32)
    half = other_ref.shape[0]
    other_ref[...] = y[:half].astype(BF)
    own_ref[...] = y[half:]
    copy.wait()


def mixer(sums, act, gate, delta_up, delta_bias, decay_log, skip_gain, order, state, wo, steps):
    rows, channels = act.shape
    n_state = decay_log.shape[0]
    width = wo.shape[1]
    vmem = pl.BlockSpec(memory_space=pltpu.VMEM)
    args = list(sums)
    args += [act, gate, delta_up, delta_bias, decay_log, skip_gain, order, state, wo]
    return pl.pallas_call(
        functools.partial(mixer_kernel, steps, n_state, len(sums) - 1),
        in_specs=[vmem] * len(args),
        out_specs=[pl.BlockSpec(memory_space=pl.ANY), vmem, vmem],
        out_shape=[
            jax.ShapeDtypeStruct(state.shape, F32),
            jax.ShapeDtypeStruct((rows // 2, width), BF),
            jax.ShapeDtypeStruct((rows // 2, width), F32),
        ],
        scratch_shapes=[
            pltpu.VMEM(state.shape, F32),
            pltpu.VMEM((rows, channels), F32),
            pltpu.SemaphoreType.DMA,
        ],
        compiler_params=pltpu.CompilerParams(vmem_limit_bytes=16 << 20),
        cost_estimate=pl.CostEstimate(
            flops=2 * rows * channels * width,
            bytes_accessed=2 * channels * width,
            transcendentals=rows * n_state * channels,
        ),
        name="mixer",
    )(*args)


def preload_kernel(block, wg, wu, wd, g0, u0, down_ref, sems):
    copies = [
        pltpu.make_async_copy(wg.at[pl.ds(0, block), :], g0, sems.at[0]),
        pltpu.make_async_copy(wu.at[pl.ds(0, block), :], u0, sems.at[1]),
        pltpu.make_async_copy(wd, down_ref, sems.at[2]),
    ]
    for copy in copies:
        copy.start()
    for copy in copies:
        copy.wait()


def preload(wg, wu, wd, block):
    vmem = pl.BlockSpec(memory_space=pltpu.VMEM)
    hbm = pl.BlockSpec(memory_space=pl.ANY)
    width = wg.shape[1]
    return pl.pallas_call(
        functools.partial(preload_kernel, block),
        in_specs=[hbm] * 3,
        out_specs=[vmem] * 3,
        out_shape=[jax.ShapeDtypeStruct((block, width), BF)] * 2
        + [jax.ShapeDtypeStruct(wd.shape, BF)],
        scratch_shapes=[pltpu.SemaphoreType.DMA((3,))],
        compiler_params=pltpu.CompilerParams(vmem_limit_bytes=PRELOAD_LIMIT),
        cost_estimate=pl.CostEstimate(
            flops=0, bytes_accessed=4 * (2 * block * width + wd.size), transcendentals=0
        ),
        name="preload",
    )(wg, wu, wd)


def experts_kernel(pieces, experts, local_experts, block, first_ref, *refs):
    held = refs[:pieces]
    g0, u0, wg, wu, act = refs[pieces : pieces + 5]
    x, tail, ring, sems = refs[pieces + 5 :]
    hidden, width = wg.shape
    rows = held[0].shape[0]
    slots = ring.shape[0]
    up_steps = hidden // block

    def fetch(i, j):
        slot = lax.rem(i, slots)
        source = (wg, wu)[j]
        return pltpu.make_async_copy(
            source.at[pl.ds(i * block, block), :], ring.at[slot, j], sems.at[slot, j]
        )

    for i in range(1, min(slots + 1, up_steps)):
        fetch(i, 0).start()
        fetch(i, 1).start()
    for i in range(pieces):
        x[i * rows : (i + 1) * rows, :] = held[i][:, :width]
        tail[i * rows : (i + 1) * rows, :] = held[i][:, width:].astype(F32)
    lane = lax.broadcasted_iota(jnp.int32, tail.shape, 1)
    per_expert = up_steps // local_experts

    def activate(i, g, u):
        expert = first_ref[0] + i // per_expert
        chosen = (lane == expert) | (lane == expert + experts)
        weight = jnp.sum(jnp.where(chosen, tail[...], 0.0), axis=1, keepdims=True)
        return (g * jax.nn.sigmoid(g) * u * weight).astype(BF)

    g = lax.dot_general(x[...], g0[...], NT, preferred_element_type=F32)
    u = lax.dot_general(x[...], u0[...], NT, preferred_element_type=F32)
    act[:, :block] = activate(0, g, u)

    def up_step(i, carry):
        slot = lax.rem(i, slots)
        fetch(i, 0).wait()
        g = lax.dot_general(x[...], ring[slot, 0], NT, preferred_element_type=F32)
        fetch(i, 1).wait()
        u = lax.dot_general(x[...], ring[slot, 1], NT, preferred_element_type=F32)
        act[:, pl.ds(pl.multiple_of(i * block, block), block)] = activate(i, g, u)

        @pl.when(i + slots < up_steps)
        def _():
            fetch(i + slots, 0).start()
            fetch(i + slots, 1).start()

        return carry

    lax.fori_loop(1, up_steps, up_step, 0)


def down_kernel(offset, cols, act, wd, own_ref, other_ref):
    half = own_ref.shape[0]

    def step(i, carry):
        here = pl.ds(pl.multiple_of(i * cols, cols), cols)
        there = pl.ds(pl.multiple_of(offset + i * cols, cols), cols)
        y = jnp.dot(act[...], wd[:, there], preferred_element_type=F32).astype(BF)
        own_ref[:, here] = y[:half]
        other_ref[:, here] = y[half:]
        return carry

    lax.fori_loop(0, own_ref.shape[1] // cols, step, 0)


def up_block(hidden, local_experts):
    block = hidden // local_experts
    while block > 512:
        block //= 2
    return block


def expert_outputs(held, first, ready, wg, wu, experts, local_experts, chunks):
    pieces, rows = len(held), held[0].shape[0]
    hidden, width = wg.shape
    total = pieces * rows
    block = up_block(hidden, local_experts)
    cols = 512
    slots = 2
    vmem = pl.BlockSpec(memory_space=pltpu.VMEM)
    hbm = pl.BlockSpec(memory_space=pl.ANY)
    g0, u0, wd = ready
    act = pl.pallas_call(
        functools.partial(experts_kernel, pieces, experts, local_experts, block),
        in_specs=[pl.BlockSpec(memory_space=pltpu.SMEM)] + [vmem] * (pieces + 2) + [hbm] * 2,
        out_specs=vmem,
        out_shape=jax.ShapeDtypeStruct((total, hidden), BF),
        scratch_shapes=[
            pltpu.VMEM((total, width), BF),
            pltpu.VMEM((total, held[0].shape[1] - width), F32),
            pltpu.VMEM((slots, 2, block, width), BF),
            pltpu.SemaphoreType.DMA((slots, 2)),
        ],
        compiler_params=pltpu.CompilerParams(vmem_limit_bytes=EXPERTS_LIMIT),
        cost_estimate=pl.CostEstimate(
            flops=4 * total * hidden * width,
            bytes_accessed=4 * hidden * width,
            transcendentals=total * hidden,
        ),
        name="experts",
    )(first, *held, g0, u0, wg, wu)
    outs = []
    part = width // chunks
    for c in range(chunks):
        outs += pl.pallas_call(
            functools.partial(down_kernel, c * part, cols),
            in_specs=[vmem] * 2,
            out_specs=[vmem] * 2,
            out_shape=[jax.ShapeDtypeStruct((total // 2, part), BF)] * 2,
            compiler_params=pltpu.CompilerParams(vmem_limit_bytes=DOWN_LIMIT),
            cost_estimate=pl.CostEstimate(
                flops=2 * total * hidden * part,
                bytes_accessed=2 * hidden * part,
                transcendentals=0,
            ),
            name=f"down_{c}",
        )(act, wd)
    return outs


def shards(
    layer_in,
    conv_state,
    ssm_state,
    proj_inner,
    proj_gate,
    conv_weight,
    conv_bias,
    delta_down,
    state_proj,
    delta_up,
    delta_bias,
    decay_log,
    skip_gain,
    proj_out,
    expert_gate,
    expert_up,
    expert_down,
    expert_ids,
    route_weight,
):
    steps, group_rows, width = layer_in.shape
    row_dev, top = expert_ids.shape[1:]
    planes = lax.axis_size("dp")
    group = lax.axis_size(PLANE)
    local_experts, hidden_dev = expert_gate.shape[:2]
    experts = local_experts * lax.axis_size("expert")
    place = lax.axis_index(PLANE)
    rank = delta_down.shape[1]
    n_state = decay_log.shape[0]
    chunks = 2

    sums, act_all, conv_final, scale = head(
        layer_in,
        proj_inner,
        jnp.transpose(conv_state, (1, 0, 2)),
        conv_weight,
        conv_bias[None],
        delta_down,
        state_proj.reshape(2 * n_state, -1),
    )
    conv_final = jnp.transpose(conv_final, (1, 0, 2))
    pair = (sums.astype(F32) + swap(sums, PLANE, group, 1).astype(F32)).astype(BF)
    layer_rows, pair = lax.optimization_barrier((layer_in.reshape(-1, width), pair))
    sums = [pair] + [swap(pair, PLANE, group, mask) for mask in range(2, group, 2)]
    gate = jax.nn.silu(jnp.dot(layer_rows, proj_gate, preferred_element_type=F32) * scale)

    own = steps * row_dev
    row = lax.broadcasted_iota(jnp.int32, (group * own, steps * group_rows), 0)
    source = lax.broadcasted_iota(jnp.int32, (group * own, steps * group_rows), 1)
    half = group // 2
    distance = 2 * (row // own % half) + (row // own < half).astype(jnp.int32)
    device = jnp.bitwise_xor(distance, place)
    wanted = (row % own) // row_dev * group_rows + device * row_dev + row % row_dev
    order = (source == wanted).astype(BF)
    channels = proj_inner.shape[1]
    new_state, mix_other, mix_own = mixer(
        sums,
        act_all,
        gate,
        delta_up,
        delta_bias[None],
        decay_log,
        skip_gain[None],
        order,
        ssm_state.reshape(group_rows * n_state, channels),
        proj_out,
        steps,
    )
    ssm_state = new_state.reshape(ssm_state.shape)
    pair = mix_own + swap(mix_other, PLANE, group, 1).astype(F32)
    mixer_out = pair[:own]
    for q in range(1, group // 2):
        block = pair[q * own : (q + 1) * own].astype(BF)
        mixer_out = mixer_out + swap(block, PLANE, group, 2 * q).astype(F32)
    own_rows = lax.dynamic_slice_in_dim(layer_in, place * row_dev, row_dev, 1)
    residual = own_rows.reshape(own, width).astype(F32) + mixer_out
    expert_in = rms_rows(residual, 1e-06).astype(BF)

    ids = expert_ids.reshape(own, top)
    table = jnp.sum(
        jnp.where(
            ids[:, :, None] == jnp.arange(experts, dtype=jnp.int32),
            route_weight.reshape(own, top)[:, :, None],
            0.0,
        ),
        axis=1,
    )
    high = table.astype(BF)
    low = (table - high.astype(F32)).astype(BF)
    extra = jnp.concatenate([high, low, jnp.zeros((own, 128 - 2 * experts), BF)], axis=1)

    block = jnp.concatenate([expert_in, extra], axis=1)
    along = {z: swap(block, "dp", planes, z) for z in range(1, planes)}
    line = jnp.concatenate([block] + [along[z] for z in range(1, planes)], axis=0)
    wg = expert_gate.reshape(local_experts * hidden_dev, width)
    wu = expert_up.reshape(local_experts * hidden_dev, width)
    wd = expert_down.reshape(local_experts * hidden_dev, width)
    line, wd = lax.optimization_barrier((line, wd))
    wg, wu, wd = [pltpu.with_memory_space_constraint(array, pltpu.HBM) for array in (wg, wu, wd)]
    ready = preload(wg, wu, wd, up_block(local_experts * hidden_dev, local_experts))
    held = [swap(line, PLANE, group, 2 * q) for q in range(1, group // 2)]
    held, ready = lax.optimization_barrier((held, ready))
    held = [line] + held
    held = held + [swap(piece, PLANE, group, 1) for piece in held]
    parts = expert_outputs(
        held,
        (lax.axis_index("expert") * local_experts)[None].astype(jnp.int32),
        ready,
        wg,
        wu,
        experts,
        local_experts,
        chunks,
    )

    line_rows = planes * own
    lines = []
    for c in range(chunks):
        mine, other = parts[2 * c : 2 * c + 2]
        pair = mine.astype(F32) + swap(other, PLANE, group, 1).astype(F32)
        line = pair[:line_rows]
        for q in range(1, group // 2):
            block = pair[q * line_rows : (q + 1) * line_rows].astype(BF)
            line = line + swap(block, PLANE, group, 2 * q).astype(F32)
        values = [line[:own]]
        for z in range(1, planes):
            block = line[z * own : (z + 1) * own].astype(BF)
            values.append(swap(block, "dp", planes, z))
        lines.append(values)
    layer_out = finish(residual, lines, steps)
    return (layer_out, conv_final, ssm_state)


def solution(mesh):
    placed = (
        P(None, "dp", None),
        P("dp", None, PLANE),
        P("dp", None, PLANE),
        P(None, PLANE),
        P(None, PLANE),
        P(None, PLANE),
        P(PLANE),
        P(PLANE, None),
        P(None, None, PLANE),
        P(None, PLANE),
        P(PLANE),
        P(None, PLANE),
        P(PLANE),
        P(PLANE, None),
        P("expert", ("dp", "tensor"), None),
        P("expert", ("dp", "tensor"), None),
        P("expert", ("dp", "tensor"), None),
        P(None, ("dp", "expert", "tensor"), None),
        P(None, ("dp", "expert", "tensor"), None),
    )
    return jax.shard_map(
        shards,
        mesh=mesh,
        in_specs=placed,
        out_specs=(
            P(None, ("dp", "expert", "tensor"), None),
            P("dp", None, PLANE),
            P("dp", None, PLANE),
        ),
        check_vma=False,
    )
```

```python
import functools

import jax
import jax.numpy as jnp
from jax import lax
from jax.experimental import pallas as pl
from jax.experimental.pallas import tpu as pltpu
from jax.sharding import PartitionSpec as P


BF = jnp.bfloat16
F32 = jnp.float32
PLANE = ("expert", "tensor")
NT = (((1,), (1,)), ((), ()))
EXPERTS_LIMIT = 28 << 20
PRELOAD_LIMIT = 4 << 20
DOWN_LIMIT = 8 << 20


def rms_rows(values, eps):
    return values * lax.rsqrt(jnp.mean(values * values, axis=-1, keepdims=True) + eps)


def swap(value, axes, size, mask):
    return lax.ppermute(value, axes, [(i, i ^ mask) for i in range(size)])


def head_kernel(
    steps, taps, parts,
    x_hbm, w_hbm, state_hbm, cw_hbm, cb_hbm, dd_hbm, sp_hbm,
    sums_ref, act_ref, conv_ref, scale_ref,
    x_ref, w_ref, state_ref, cw_ref, cb_ref, dd_ref, sp_ref, sems,
):
    group_rows, width = x_hbm.shape[1:]
    block = width // parts
    copies = [pltpu.make_async_copy(x_hbm, x_ref, sems.at[0])]
    for k in range(parts):
        rows = pl.ds(k * block, block)
        copies.append(pltpu.make_async_copy(w_hbm.at[rows], w_ref.at[rows], sems.at[1 + k]))
    rest = (
        (state_hbm, state_ref),
        (cw_hbm, cw_ref),
        (cb_hbm, cb_ref),
        (dd_hbm, dd_ref),
        (sp_hbm, sp_ref),
    )
    for i, (source, target) in enumerate(rest):
        copies.append(pltpu.make_async_copy(source, target, sems.at[1 + parts + i]))
    for copy in copies:
        copy.start()
    copies[0].wait()
    x = x_ref[...].reshape(steps * group_rows, width)
    x_float = x.astype(F32)
    scale = lax.rsqrt(jnp.mean(x_float * x_float, axis=1, keepdims=True) + 1e-06)
    scale_ref[...] = scale
    acc = None
    for k in range(parts):
        copies[1 + k].wait()
        part = jnp.dot(
            x[:, k * block : (k + 1) * block],
            w_ref[k * block : (k + 1) * block, :],
            preferred_element_type=F32,
        )
        acc = part if acc is None else acc + part
    conv_input = (acc * scale).astype(BF)
    for copy in copies[1 + parts :]:
        copy.wait()
    history = [state_ref[i] for i in range(taps - 1)]
    history += [conv_input[s * group_rows : (s + 1) * group_rows] for s in range(steps)]
    for i in range(taps - 1):
        conv_ref[i] = history[steps + i]
    for s in range(steps):
        total = cb_ref[...] + sum(
            history[s + i].astype(F32) * cw_ref[i : i + 1, :] for i in range(taps)
        )
        act_ref[s * group_rows : (s + 1) * group_rows, :] = (
            total * jax.nn.sigmoid(total)
        ).astype(BF)
    act = act_ref[...]
    rank = dd_ref.shape[1]
    sums_ref[:, :rank] = jnp.dot(act, dd_ref[...], preferred_element_type=F32).astype(BF)
    sums_ref[:, rank:] = lax.dot_general(
        act, sp_ref[...], NT, preferred_element_type=F32
    ).astype(BF)


def head(layer_in, proj_inner, conv_state, conv_weight, conv_bias, delta_down, state_proj):
    steps, group_rows, _ = layer_in.shape
    rows = steps * group_rows
    channels = proj_inner.shape[1]
    rank = delta_down.shape[1]
    n_sums = state_proj.shape[0]
    parts = 4
    args = [layer_in, proj_inner, conv_state, conv_weight, conv_bias, delta_down, state_proj]
    outs = [
        jax.ShapeDtypeStruct((rows, rank + n_sums), BF),
        jax.ShapeDtypeStruct((rows, channels), BF),
        jax.ShapeDtypeStruct(conv_state.shape, BF),
        jax.ShapeDtypeStruct((rows, 1), F32),
    ]
    return pl.pallas_call(
        functools.partial(head_kernel, steps, conv_weight.shape[0], parts),
        in_specs=[pl.BlockSpec(memory_space=pl.ANY)] * len(args),
        out_specs=[pl.BlockSpec(memory_space=pltpu.VMEM)] * len(outs),
        out_shape=outs,
        scratch_shapes=[pltpu.VMEM(array.shape, array.dtype) for array in args]
        + [pltpu.SemaphoreType.DMA((parts + len(args) - 1,))],
        compiler_params=pltpu.CompilerParams(vmem_limit_bytes=16 << 20),
        name="head",
    )(*[pltpu.with_memory_space_constraint(array, pltpu.HBM) for array in args])


def finish_kernel(chunks, residual_ref, *refs):
    out_ref = refs[-1]
    each = out_ref.shape[1]
    per_chunk = (len(refs) - 1) // chunks
    for c in range(chunks):
        parts = refs[c * per_chunk : (c + 1) * per_chunk]
        cols = parts[0].shape[1]
        here = slice(c * cols, (c + 1) * cols)
        rows = residual_ref[:, here]
        for ref in parts:
            rows = rows + ref[...].astype(F32)
        rows = rows.astype(BF)
        for s in range(out_ref.shape[0]):
            out_ref[s, :, here] = rows[s * each : (s + 1) * each]


def finish(residual, chunks, steps):
    rows, width = residual.shape
    return pl.pallas_call(
        functools.partial(finish_kernel, len(chunks)),
        out_shape=jax.ShapeDtypeStruct((steps, rows // steps, width), BF),
        compiler_params=pltpu.CompilerParams(vmem_limit_bytes=4 << 20),
        name="finish",
    )(residual, *[value for chunk in chunks for value in chunk])


def mixer_kernel(steps, n_state, received, *refs):
    sums = refs[: 1 + received]
    (
        act_ref, gate_ref, du_ref, db_ref, dl_ref, sg_ref, order_ref, st_ref, wo_ref,
        new_hbm, other_ref, own_ref, new_ref, read_ref, sem,
    ) = refs[1 + received :]
    total = sum(ref[...].astype(F32) for ref in sums)
    rank = du_ref.shape[0]
    low = total[:, :rank]
    scale = lax.rsqrt(jnp.mean(low * low, axis=1, keepdims=True) + 1e-06)
    raw = jnp.dot((low * scale).astype(BF), du_ref[...], preferred_element_type=F32) + db_ref[...]
    step_size = jnp.maximum(raw, 0.0) + jnp.log1p(jnp.exp(-jnp.abs(raw)))
    act = act_ref[...].astype(F32)
    rate = jnp.exp(dl_ref[...])
    rows = act.shape[0] // steps
    drive = step_size * act
    columns = total[:, rank:].T
    for r in range(rows):
        where = slice(r * n_state, (r + 1) * n_state)
        state = st_ref[where, :]
        for s in range(steps):
            i = s * rows + r
            decay = jnp.exp(-step_size[i : i + 1] * rate)
            state = decay * state + drive[i : i + 1] * columns[:n_state, i : i + 1]
            read_ref[i : i + 1, :] = jnp.sum(
                state * columns[n_state:, i : i + 1], axis=0, keepdims=True
            )
        new_ref[where, :] = state
    gated = ((read_ref[...] + sg_ref[...] * act) * gate_ref[...]).astype(BF)
    copy = pltpu.make_async_copy(new_ref, new_hbm, sem)
    copy.start()
    gated = jnp.dot(order_ref[...], gated, preferred_element_type=F32).astype(BF)
    y = jnp.dot(gated, wo_ref[...], preferred_element_type=F32)
    half = other_ref.shape[0]
    other_ref[...] = y[:half].astype(BF)
    own_ref[...] = y[half:]
    copy.wait()


def mixer(sums, act, gate, delta_up, delta_bias, decay_log, skip_gain, order, state, wo, steps):
    rows, channels = act.shape
    n_state = decay_log.shape[0]
    width = wo.shape[1]
    vmem = pl.BlockSpec(memory_space=pltpu.VMEM)
    args = list(sums)
    args += [act, gate, delta_up, delta_bias, decay_log, skip_gain, order, state, wo]
    return pl.pallas_call(
        functools.partial(mixer_kernel, steps, n_state, len(sums) - 1),
        in_specs=[vmem] * len(args),
        out_specs=[pl.BlockSpec(memory_space=pl.ANY), vmem, vmem],
        out_shape=[
            jax.ShapeDtypeStruct(state.shape, F32),
            jax.ShapeDtypeStruct((rows // 2, width), BF),
            jax.ShapeDtypeStruct((rows // 2, width), F32),
        ],
        scratch_shapes=[
            pltpu.VMEM(state.shape, F32),
            pltpu.VMEM((rows, channels), F32),
            pltpu.SemaphoreType.DMA,
        ],
        compiler_params=pltpu.CompilerParams(vmem_limit_bytes=16 << 20),
        cost_estimate=pl.CostEstimate(
            flops=2 * rows * channels * width,
            bytes_accessed=2 * channels * width,
            transcendentals=rows * n_state * channels,
        ),
        name="mixer",
    )(*args)


def preload_kernel(block, wg, wu, wd, g0, u0, down_ref, sems):
    copies = [
        pltpu.make_async_copy(wg.at[pl.ds(0, block), :], g0, sems.at[0]),
        pltpu.make_async_copy(wu.at[pl.ds(0, block), :], u0, sems.at[1]),
        pltpu.make_async_copy(wd, down_ref, sems.at[2]),
    ]
    for copy in copies:
        copy.start()
    for copy in copies:
        copy.wait()


def preload(wg, wu, wd, block):
    vmem = pl.BlockSpec(memory_space=pltpu.VMEM)
    hbm = pl.BlockSpec(memory_space=pl.ANY)
    width = wg.shape[1]
    return pl.pallas_call(
        functools.partial(preload_kernel, block),
        in_specs=[hbm] * 3,
        out_specs=[vmem] * 3,
        out_shape=[jax.ShapeDtypeStruct((block, width), BF)] * 2
        + [jax.ShapeDtypeStruct(wd.shape, BF)],
        scratch_shapes=[pltpu.SemaphoreType.DMA((3,))],
        compiler_params=pltpu.CompilerParams(vmem_limit_bytes=PRELOAD_LIMIT),
        cost_estimate=pl.CostEstimate(
            flops=0, bytes_accessed=4 * (2 * block * width + wd.size), transcendentals=0
        ),
        name="preload",
    )(wg, wu, wd)


def experts_kernel(pieces, experts, local_experts, block, first_ref, *refs):
    held = refs[:pieces]
    g0, u0, wg, wu, act = refs[pieces : pieces + 5]
    x, tail, ring, sems = refs[pieces + 5 :]
    hidden, width = wg.shape
    rows = held[0].shape[0]
    slots = ring.shape[0]
    up_steps = hidden // block

    def fetch(i, j):
        slot = lax.rem(i, slots)
        source = (wg, wu)[j]
        return pltpu.make_async_copy(
            source.at[pl.ds(i * block, block), :], ring.at[slot, j], sems.at[slot, j]
        )

    for i in range(1, min(slots + 1, up_steps)):
        fetch(i, 0).start()
        fetch(i, 1).start()
    for i in range(pieces):
        x[i * rows : (i + 1) * rows, :] = held[i][:, :width]
        tail[i * rows : (i + 1) * rows, :] = held[i][:, width:].astype(F32)
    lane = lax.broadcasted_iota(jnp.int32, tail.shape, 1)
    per_expert = up_steps // local_experts

    def activate(i, g, u):
        expert = first_ref[0] + i // per_expert
        chosen = (lane == expert) | (lane == expert + experts)
        weight = jnp.sum(jnp.where(chosen, tail[...], 0.0), axis=1, keepdims=True)
        return (g * jax.nn.sigmoid(g) * u * weight).astype(BF)

    g = lax.dot_general(x[...], g0[...], NT, preferred_element_type=F32)
    u = lax.dot_general(x[...], u0[...], NT, preferred_element_type=F32)
    act[:, :block] = activate(0, g, u)

    def up_step(i, carry):
        slot = lax.rem(i, slots)
        fetch(i, 0).wait()
        g = lax.dot_general(x[...], ring[slot, 0], NT, preferred_element_type=F32)
        fetch(i, 1).wait()
        u = lax.dot_general(x[...], ring[slot, 1], NT, preferred_element_type=F32)
        act[:, pl.ds(pl.multiple_of(i * block, block), block)] = activate(i, g, u)

        @pl.when(i + slots < up_steps)
        def _():
            fetch(i + slots, 0).start()
            fetch(i + slots, 1).start()

        return carry

    lax.fori_loop(1, up_steps, up_step, 0)


def down_kernel(offset, cols, act, wd, own_ref, other_ref):
    half = own_ref.shape[0]

    def step(i, carry):
        here = pl.ds(pl.multiple_of(i * cols, cols), cols)
        there = pl.ds(pl.multiple_of(offset + i * cols, cols), cols)
        y = jnp.dot(act[...], wd[:, there], preferred_element_type=F32).astype(BF)
        own_ref[:, here] = y[:half]
        other_ref[:, here] = y[half:]
        return carry

    lax.fori_loop(0, own_ref.shape[1] // cols, step, 0)


def up_block(hidden, local_experts):
    block = hidden // local_experts
    while block > 512:
        block //= 2
    return block


def expert_outputs(held, first, ready, wg, wu, experts, local_experts, chunks):
    pieces, rows = len(held), held[0].shape[0]
    hidden, width = wg.shape
    total = pieces * rows
    block = up_block(hidden, local_experts)
    cols = 512
    slots = 2
    vmem = pl.BlockSpec(memory_space=pltpu.VMEM)
    hbm = pl.BlockSpec(memory_space=pl.ANY)
    g0, u0, wd = ready
    act = pl.pallas_call(
        functools.partial(experts_kernel, pieces, experts, local_experts, block),
        in_specs=[pl.BlockSpec(memory_space=pltpu.SMEM)] + [vmem] * (pieces + 2) + [hbm] * 2,
        out_specs=vmem,
        out_shape=jax.ShapeDtypeStruct((total, hidden), BF),
        scratch_shapes=[
            pltpu.VMEM((total, width), BF),
            pltpu.VMEM((total, held[0].shape[1] - width), F32),
            pltpu.VMEM((slots, 2, block, width), BF),
            pltpu.SemaphoreType.DMA((slots, 2)),
        ],
        compiler_params=pltpu.CompilerParams(vmem_limit_bytes=EXPERTS_LIMIT),
        cost_estimate=pl.CostEstimate(
            flops=4 * total * hidden * width,
            bytes_accessed=4 * hidden * width,
            transcendentals=total * hidden,
        ),
        name="experts",
    )(first, *held, g0, u0, wg, wu)
    outs = []
    part = width // chunks
    for c in range(chunks):
        outs += pl.pallas_call(
            functools.partial(down_kernel, c * part, cols),
            in_specs=[vmem] * 2,
            out_specs=[vmem] * 2,
            out_shape=[jax.ShapeDtypeStruct((total // 2, part), BF)] * 2,
            compiler_params=pltpu.CompilerParams(vmem_limit_bytes=DOWN_LIMIT),
            cost_estimate=pl.CostEstimate(
                flops=2 * total * hidden * part,
                bytes_accessed=2 * hidden * part,
                transcendentals=0,
            ),
        )(act, wd)
    return outs


def shards(
    layer_in,
    conv_state,
    ssm_state,
    proj_inner,
    proj_gate,
    conv_weight,
    conv_bias,
    delta_down,
    state_proj,
    delta_up,
    delta_bias,
    decay_log,
    skip_gain,
    proj_out,
    expert_gate,
    expert_up,
    expert_down,
    expert_ids,
    route_weight,
):
    steps, group_rows, width = layer_in.shape
    row_dev, top = expert_ids.shape[1:]
    planes = lax.axis_size("dp")
    group = lax.axis_size(PLANE)
    local_experts, hidden_dev = expert_gate.shape[:2]
    experts = local_experts * lax.axis_size("expert")
    place = lax.axis_index(PLANE)
    n_state = decay_log.shape[0]
    chunks = 2

    sums, act_all, conv_final, scale = head(
        layer_in,
        proj_inner,
        jnp.transpose(conv_state, (1, 0, 2)),
        conv_weight,
        conv_bias[None],
        delta_down,
        state_proj.reshape(2 * n_state, -1),
    )
    conv_final = jnp.transpose(conv_final, (1, 0, 2))
    pair = (sums.astype(F32) + swap(sums, PLANE, group, 1).astype(F32)).astype(BF)
    layer_rows, pair = lax.optimization_barrier((layer_in.reshape(-1, width), pair))
    sums = [pair] + [swap(pair, PLANE, group, mask) for mask in range(2, group, 2)]
    gate = jax.nn.silu(jnp.dot(layer_rows, proj_gate, preferred_element_type=F32) * scale)

    own = steps * row_dev
    row = lax.broadcasted_iota(jnp.int32, (group * own, steps * group_rows), 0)
    source = lax.broadcasted_iota(jnp.int32, (group * own, steps * group_rows), 1)
    half = group // 2
    distance = 2 * (row // own % half) + (row // own < half).astype(jnp.int32)
    device = jnp.bitwise_xor(distance, place)
    wanted = (row % own) // row_dev * group_rows + device * row_dev + row % row_dev
    order = (source == wanted).astype(BF)
    channels = proj_inner.shape[1]
    new_state, mix_other, mix_own = mixer(
        sums,
        act_all,
        gate,
        delta_up,
        delta_bias[None],
        decay_log,
        skip_gain[None],
        order,
        ssm_state.reshape(group_rows * n_state, channels),
        proj_out,
        steps,
    )
    ssm_state = new_state.reshape(ssm_state.shape)
    pair = mix_own + swap(mix_other, PLANE, group, 1).astype(F32)
    mixer_out = pair[:own]
    for q in range(1, group // 2):
        block = pair[q * own : (q + 1) * own].astype(BF)
        received = swap(block, PLANE, group, 2 * q)
        mixer_out = mixer_out + received.astype(F32)
    own_rows = lax.dynamic_slice_in_dim(layer_in, place * row_dev, row_dev, 1)
    residual = own_rows.reshape(own, width).astype(F32) + mixer_out
    expert_in = rms_rows(residual, 1e-06).astype(BF)

    ids = expert_ids.reshape(own, top)
    table = jnp.sum(
        jnp.where(
            ids[:, :, None] == jnp.arange(experts, dtype=jnp.int32),
            route_weight.reshape(own, top)[:, :, None],
            0.0,
        ),
        axis=1,
    )
    high = table.astype(BF)
    low = (table - high.astype(F32)).astype(BF)
    extra = jnp.concatenate([high, low, jnp.zeros((own, 128 - 2 * experts), BF)], axis=1)

    block = jnp.concatenate([expert_in, extra], axis=1)
    along = {z: swap(block, "dp", planes, z) for z in range(1, planes)}
    line = jnp.concatenate([block] + [along[z] for z in range(1, planes)], axis=0)
    wg = expert_gate.reshape(local_experts * hidden_dev, width)
    wu = expert_up.reshape(local_experts * hidden_dev, width)
    wd = expert_down.reshape(local_experts * hidden_dev, width)
    line, wd = lax.optimization_barrier((line, wd))
    wg, wu, wd = [pltpu.with_memory_space_constraint(array, pltpu.HBM) for array in (wg, wu, wd)]
    ready = preload(wg, wu, wd, up_block(local_experts * hidden_dev, local_experts))
    held = [swap(line, PLANE, group, 2 * q) for q in range(1, group // 2)]
    held, ready = lax.optimization_barrier((held, ready))
    held = [line] + held
    held = held + [swap(piece, PLANE, group, 1) for piece in held]
    parts = expert_outputs(
        held,
        (lax.axis_index("expert") * local_experts)[None].astype(jnp.int32),
        ready,
        wg,
        wu,
        experts,
        local_experts,
        chunks,
    )

    line_rows = planes * own
    lines = []
    for c in range(chunks):
        mine, other = parts[2 * c : 2 * c + 2]
        pair = mine.astype(F32) + swap(other, PLANE, group, 1).astype(F32)
        line = pair[:line_rows]
        for q in range(1, group // 2):
            block = pair[q * line_rows : (q + 1) * line_rows].astype(BF)
            received = swap(block, PLANE, group, 2 * q)
            line = line + received.astype(F32)
        values = [line[:own]]
        for z in range(1, planes):
            block = line[z * own : (z + 1) * own].astype(BF)
            values.append(swap(block, "dp", planes, z))
        lines.append(values)
    layer_out = finish(residual, lines, steps)
    return (layer_out, conv_final, ssm_state)


def solution(mesh):
    placed = (
        P(None, "dp", None),
        P("dp", None, PLANE),
        P("dp", None, PLANE),
        P(None, PLANE),
        P(None, PLANE),
        P(None, PLANE),
        P(PLANE),
        P(PLANE, None),
        P(None, None, PLANE),
        P(None, PLANE),
        P(PLANE),
        P(None, PLANE),
        P(PLANE),
        P(PLANE, None),
        P("expert", ("dp", "tensor"), None),
        P("expert", ("dp", "tensor"), None),
        P("expert", ("dp", "tensor"), None),
        P(None, ("dp", "expert", "tensor"), None),
        P(None, ("dp", "expert", "tensor"), None),
    )
    return jax.shard_map(
        shards,
        mesh=mesh,
        in_specs=placed,
        out_specs=(
            P(None, ("dp", "expert", "tensor"), None),
            P("dp", None, PLANE),
            P("dp", None, PLANE),
        ),
        check_vma=False,
    )
```
